512 devices in a mesh: req: 64 (over z, x, core), tensor: 8 (over y).
Axes of the slice: x: 4, y: 8, z: 8, core: 2. Of those that a mesh axis runs over, the one named last changes fastest.
Arguments:
- tokens: bfloat16 [4096, 1024], P('req'), may hold values from -6 to 6
- norm_gain: float32 [1024], replicated, may hold values from 0.1 to 1.9
- w_qkv: bfloat16 [1024, 3, 1024], P(None, None, 'tensor'), may hold values from -0.1875 to 0.1875
- w_out: bfloat16 [1024, 1024], P('tensor'), may hold values from -0.25 to 0.25
- root_kv: bfloat16 [4096, 2, 1024], P('req', None, 'tensor'), may hold values from -60 to 60, as said below
- branch_kv: bfloat16 [64, 1024, 2, 1024], P('req', None, None, 'tensor'), may hold values from -60 to 60, as said below
- leaf_kv: bfloat16 [1024, 16, 2, 1024], P('req', None, None, 'tensor'), may hold values from -60 to 60, as said below
- branch: int32 [1024, 1], P('req'), may hold values from 0 to 63; in each aligned block of 16 rows (0 to 15, 16 to 31, ...) at most 2 rows name the same one
- node_owner: int32 [64], replicated, may hold values from 0 to 63, each once
- branch_len: int32 [64], replicated, may hold values from 1 to 1024, as said below
- leaf_len: int32 [1024], P('req'), may hold values from 1 to 16
- new_count: int32 [1024], P('req'), may hold values from 1 to 4
Outputs:
- attn_out: bfloat16 [4096, 1024], P('req', 'tensor')
The draws below stay inside these ranges and needn't reach their ends.
Inputs may be any that keep to these rules, and one draw needn't show every extreme that they name: Among the 16 requests of one device (aligned blocks of rows) no branch node is named more than 2 times; some node is named exactly 2 times. `node_owner`: each storage slot holds exactly one node. `branch_len`: some node has all 1024 positions. `root_kv`: Real-valued keys and values. `branch_kv`: Real-valued keys and values. `leaf_kv`: Real-valued keys and values.
All inputs are finite; a program needn't handle non-finite values.
Results may differ from the reference program's by a relative error of at most 0.0095.
The reference program's roundings to bfloat16 on the way count: a program that leaves them out, or rounds other values in their place, can miss the bound.
Values may be sent and summed in bfloat16 or wider, within the bound.
No kernel may reach another device: no remote copies, remote signals or barrier semaphores. Data moves between devices by JAX's collectives and lax.ppermute only.
A program may use at most 64 MiB of HBM per device.

```python
import math
import jax
import jax.numpy as jnp
import numpy as np
from jax import lax

D = 1024
H = 16
HD = 64
NEWMAX = 4
REQ_DEV = 16
LEN1 = 1024
LEN2 = 16
REQUESTS = 1024
ROWS = 4096
ROOT = 4096
NODES = 64
CAP = 2


def cache_draw(key, shape):
    key_one, key_two = jax.random.split(key, 2)
    half_shape = shape[:-2] + (1, shape[-1])
    key_part = jnp.clip(3.0 * jax.random.normal(key_one, half_shape, jnp.float32), -16.0, 16.0)
    value_part = jnp.clip(jax.random.normal(key_two, half_shape, jnp.float32), -6.0, 6.0)
    return jnp.concatenate([key_part, value_part], axis=-2).astype(jnp.bfloat16)


def draw_root_kv(key, part):
    return cache_draw(jax.random.fold_in(key, 11), (ROOT, 2, H * HD))


def draw_branch_kv(key, part):
    return cache_draw(jax.random.fold_in(key, 12), (NODES, LEN1, 2, H * HD))


def draw_leaf_kv(key, part):
    return cache_draw(jax.random.fold_in(key, 13), (REQUESTS, LEN2, 2, H * HD))


def draw_branch_len(key, part):
    key_one, key_two = jax.random.split(jax.random.fold_in(key, 14))
    lengths = jax.random.randint(key_one, (NODES,), 1, LEN1 + 1)
    longest = jax.random.randint(key_two, (), 0, NODES)
    return lengths.at[longest].set(LEN1).astype(jnp.int32)


def plant(entries, stream_key, least, high):
    spot = [jax.random.randint(jax.random.fold_in(stream_key, axis), (), 0, length) for axis, length in enumerate(entries.shape)]
    widest = entries.shape.index(max(entries.shape))
    beside = spot[:widest] + [(spot[widest] + 1) % entries.shape[widest]] + spot[widest + 1:]
    return entries.at[tuple(spot)].set(least).at[tuple(beside)].set(high)


def strengthened(values, rng, source, target, blocks, factor):
    owner, partner = [(jnp.arange(values.shape[position]) // (values.shape[position] // blocks)).reshape([-1 if axis == position else 1 for axis in range(values.ndim)]) for position in (source, target)]
    chosen = jax.random.permutation(rng, blocks)[partner]
    strong = (owner == chosen) | (owner == (partner + blocks // 2) % blocks)
    return jnp.where(strong, factor * values, values)


def level_of(stream_key, shape, pieces, least, high):
    factor_of = 1.0
    for dim, blocks in pieces:
        heights = jax.random.uniform(jax.random.fold_in(jax.random.fold_in(stream_key, 6), dim), (blocks,), jnp.float32, least / len(pieces), high / len(pieces))
        factor_of = factor_of * jnp.repeat(jnp.exp(heights), shape[dim] // blocks).reshape((-1,) + (1,) * (len(shape) - 1 - dim))
    return factor_of


def routed_block(own_key, own, number, rows, amount, top, most, lean):
    ranking = jax.random.permutation(own_key, amount)
    crowded, usual = portions_of(amount, rows * top, most, lean, True), portions_of(amount, rows * top, most, lean, False)
    places = jnp.arange(amount)

    def named(sizes, turn):
        used = int((sizes > 0).sum())
        fixed = max(1, used // 4)
        moved = fixed + (places - fixed + turn * (used - fixed)) % max(1, amount - fixed)
        return jnp.zeros((amount,), jnp.int32).at[ranking[jnp.where(places < fixed, places, moved)]].set(jnp.asarray(sizes, jnp.int32))

    sizes = jnp.where(number % 4 == 0, named(crowded, number // 4), named(usual, number - number // 4 - 1))
    mixed = jax.random.permutation(jax.random.fold_in(own, 3), amount)
    giver, sink = mixed[0:amount // 2 * 2:2], mixed[1:amount // 2 * 2:2]
    slack = jnp.minimum(sizes[giver] - 1, most - sizes[sink]) // 2
    slack = jnp.where((giver == ranking[0]) | (sink == ranking[0]) | (sizes[sink] == 0), 0, jnp.maximum(slack, 0))
    moved = jax.random.randint(jax.random.fold_in(own, 4), (amount // 2,), 0, 1 << 20) % (slack + 1)
    sizes = sizes.at[giver].add(-moved).at[sink].add(moved)
    labels = jnp.searchsorted(jnp.cumsum(sizes), jnp.arange(rows * top), side="right").astype(jnp.int32)
    listing = labels.reshape(top, rows).T
    listing = listing[jax.random.permutation(jax.random.fold_in(own, 1), rows)]
    turn = jax.random.randint(jax.random.fold_in(own, 2), (rows, 1), 0, top)
    return jnp.take_along_axis(listing, (jnp.arange(top)[None, :] + turn) % top, axis=1)


def portions_of(number_of, total, limit, lean, full):
    portions = [(1 << 20) // math.isqrt(grade ** lean) + 1 for grade in range(1, number_of + 1)]
    largest = limit if full else min(limit, max(-(-total // number_of), total * portions[0] // sum(portions)))
    least = 1 if total - largest >= number_of - 1 else 0
    counts, spare = [largest] + [least] * (number_of - 1), total - largest - least * (number_of - 1)
    while spare > 0:
        candidates = [i for i in range(1, number_of) if counts[i] < largest] or [i for i in range(1, number_of) if counts[i] < limit]
        mass, left = sum([portions[i] for i in candidates]), spare
        for i in candidates:
            more = min(limit - counts[i], max(1, left * portions[i] // mass), spare)
            counts[i] = counts[i] + more
            spare = spare - more
    return np.array(counts)


def bell_draw(stream_key, shape, scale, bound, shards=(), dtype=jnp.bfloat16):
    result = jax.random.normal(stream_key, shape, jnp.float32) * scale
    if len(shards) > 0:
        result = level_of(stream_key, shape, shards, -0.22, 0.18) * result
    return jnp.clip(result, min=-bound, max=bound).astype(dtype)


def heavy_noise(stream_key, shape, deviation, reach, shards, heavy, kind=jnp.bfloat16):
    array = deviation * jax.random.normal(stream_key, shape, jnp.float32)
    if shards:
        array = array * level_of(stream_key, shape, shards, -0.22, 0.18)
    return jnp.clip(strengthened(array, jax.random.fold_in(stream_key, 3), *heavy), -reach, reach).astype(kind)


def setup_inputs(seed: int = 0) -> dict:
    keys = jax.random.split(jax.random.key(seed), 13)
    tokens = bell_draw(keys[0], (ROWS, D), 1.0, 6.0, ((0, 64),))
    norm_gain = jnp.clip(1.0 + 0.18 * jax.random.normal(keys[1], (D,), jnp.float32), 0.1, 1.9)
    w_qkv = bell_draw(keys[2], (D, 3, H * HD), D ** -0.5, 0.1875, ((2, 8),))
    w_out = heavy_noise(keys[3], (H * HD, D), (H * HD) ** -0.5, 0.25, ((0, 8),), (0, 1, 8, 2.0))
    root_kv = draw_root_kv(jax.random.fold_in(keys[12], 71), 0)
    branch_kv = draw_branch_kv(jax.random.fold_in(keys[12], 71), 0)
    leaf_kv = draw_leaf_kv(jax.random.fold_in(keys[12], 71), 0)
    branch_keys = jax.random.split(jax.random.fold_in(keys[7], 1), REQUESTS // REQ_DEV)
    branch_turns = jax.random.permutation(jax.random.fold_in(keys[7], 3), REQUESTS // REQ_DEV)
    branch = jax.vmap(lambda own, number: routed_block(jax.random.fold_in(keys[7], 2), own, number, REQ_DEV, NODES, 1, CAP, 2))(branch_keys, branch_turns).reshape((REQUESTS, 1))
    node_owner = jax.random.permutation(keys[8], NODES).astype(jnp.int32)
    branch_len = draw_branch_len(jax.random.fold_in(keys[12], 71), 0)
    leaf_len = plant(jax.random.randint(keys[10], (REQUESTS,), 1, LEN2 + 1), jax.random.fold_in(keys[10], 1), 1, LEN2).astype(jnp.int32)
    new_count = plant(jax.random.randint(keys[11], (REQUESTS,), 1, NEWMAX + 1), jax.random.fold_in(keys[11], 1), 1, NEWMAX).astype(jnp.int32)
    return {"tokens": tokens, "norm_gain": norm_gain, "w_qkv": w_qkv, "w_out": w_out, "root_kv": root_kv, "branch_kv": branch_kv, "leaf_kv": leaf_kv, "branch": branch, "node_owner": node_owner, "branch_len": branch_len, "leaf_len": leaf_len, "new_count": new_count}


def partial_softmax(queries, key_rows, value_rows, usable):
    scores = jnp.einsum('qhe,khe->qhk', queries.astype(jnp.float32), key_rows.astype(jnp.float32)) * HD ** (-0.5)
    masked = jnp.where(usable[:, None, :], scores, -jnp.inf)
    peak = lax.optimization_barrier(jnp.max(masked, axis=2))
    weights = jnp.where(usable[:, None, :], jnp.exp(scores - peak[:, :, None]), 0.0)
    totals = lax.optimization_barrier(jnp.sum(weights, axis=2))
    rounded = weights.astype(jnp.bfloat16).astype(jnp.float32)
    weighted = jnp.einsum('qhk,khe->qhe', rounded, value_rows.astype(jnp.float32))
    return (peak, totals, weighted)

def reference(tokens, norm_gain, w_qkv, w_out, root_kv, branch_kv, leaf_kv, branch, node_owner, branch_len, leaf_len, new_count):
    floats = tokens.astype(jnp.float32)
    normed = (floats * lax.rsqrt(lax.optimization_barrier(jnp.mean(floats * floats, axis=1, keepdims=True)) + 1e-05) * norm_gain).astype(jnp.bfloat16)
    projected = jnp.dot(normed, w_qkv.reshape(D, 3 * H * HD), preferred_element_type=jnp.float32).astype(jnp.bfloat16)
    projected = projected.reshape(REQUESTS, NEWMAX, 3, H, HD)
    root_keys = root_kv[:, 0].reshape(ROOT, H, HD)
    root_values = root_kv[:, 1].reshape(ROOT, H, HD)
    owner_slot = node_owner[branch[:, 0]].astype(jnp.int32)
    stored_len = branch_len[branch[:, 0]]
    positions = jnp.arange(LEN2 + NEWMAX)
    shifted = positions - LEN2
    draft_pos = jnp.arange(NEWMAX)
    branch_pos = jnp.arange(LEN1)

    def serve(index):
        block = projected[index]
        queries = block[:, 0]
        root_state = partial_softmax(queries, root_keys, root_values, jnp.ones((NEWMAX, ROOT), jnp.bool_))
        cache = lax.dynamic_index_in_dim(branch_kv, owner_slot[index], 0, keepdims=False)
        usable = jnp.broadcast_to(branch_pos[None, :] < stored_len[index], (NEWMAX, LEN1))
        branch_state = partial_softmax(queries, cache[:, 0].reshape(LEN1, H, HD), cache[:, 1].reshape(LEN1, H, HD), usable)
        leaf = leaf_kv[index]
        local_keys = jnp.concatenate([leaf[:, 0].reshape(LEN2, H, HD), block[:, 1]], axis=0)
        local_values = jnp.concatenate([leaf[:, 1].reshape(LEN2, H, HD), block[:, 2]], axis=0)
        local_usable = jnp.where(positions[None, :] < LEN2, positions[None, :] < leaf_len[index], (shifted[None, :] <= draft_pos[:, None]) & (shifted[None, :] < new_count[index]))
        local_state = partial_softmax(queries, local_keys, local_values, local_usable)
        states = (root_state, branch_state, local_state)
        peak = jnp.maximum(jnp.maximum(root_state[0], branch_state[0]), local_state[0])
        totals = jnp.zeros((NEWMAX, H), jnp.float32)
        weighted = jnp.zeros((NEWMAX, H, HD), jnp.float32)
        for state in states:
            factor = jnp.exp(state[0] - peak)
            totals = totals + factor * state[1]
            weighted = weighted + factor[:, :, None] * state[2]
        return (weighted / totals[:, :, None]).reshape(NEWMAX, H * HD)

    def serve_bundle(indices):
        return jax.vmap(serve)(indices)
    bundles = jnp.arange(REQUESTS).astype(jnp.int32).reshape(-1, 16)
    attention = lax.map(serve_bundle, bundles).reshape(ROWS, H * HD).astype(jnp.bfloat16)
    product = jnp.dot(attention, w_out, preferred_element_type=jnp.float32)
    in_use = (jnp.arange(NEWMAX)[None, :] < new_count[:, None]).reshape(ROWS)
    return jnp.where(in_use[:, None], product, 0.0).astype(jnp.bfloat16)
```

```python
import jax
import jax.numpy as jnp
from jax import lax
from jax.experimental import pallas as pl
from jax.experimental.pallas import tpu as pltpu
from jax.sharding import Mesh
from jax.sharding import PartitionSpec as P

HD = 64
WIDTH = 128
DRAFTS = 4
CAPACITY = 2
NEG = -1e30
F32 = jnp.float32
BF16 = jnp.bfloat16
REQ = ("z", "x", "c")
VM = pl.BlockSpec(memory_space=pltpu.VMEM)
SM = pl.BlockSpec(memory_space=pltpu.SMEM)
PARAMS = pltpu.CompilerParams(vmem_limit_bytes=48 * 1024 * 1024)


def iota(shape, dim):
    return lax.broadcasted_iota(jnp.int32, shape, dim)


def low_lanes(shape):
    return iota(shape, len(shape) - 1) < HD


def stack_heads(q):
    low = low_lanes(q.shape)
    zero = jnp.zeros_like(q)
    return jnp.concatenate([jnp.where(low, q, zero), jnp.where(low, zero, q)], axis=0)


def merge_heads(x):
    n = x.shape[0] // 2
    return jnp.where(low_lanes((n, WIDTH)), x[:n], x[n:])


def dot_nt(a, b):
    return lax.dot_general(a, b, (((1,), (1,)), ((), ())), preferred_element_type=F32)


def front_kernel(
    branch_s,
    owner_s,
    leaf_len_s,
    new_s,
    tok_ref,
    gain_ref,
    w_ref,
    leaf_k_ref,
    leaf_v_ref,
    q_ref,
    out_ref,
    m_ref,
    t_ref,
    o_ref,
    pos_ref,
    use_ref,
    count_s,
):
    rows = tok_ref.shape[0]
    requests = rows // DRAFTS
    x = tok_ref[...].astype(F32)
    scale = lax.rsqrt(jnp.mean(x * x, axis=1, keepdims=True) + 1e-05)
    normed = (x * scale * gain_ref[...]).astype(BF16)
    projected = jnp.dot(normed, w_ref[...], preferred_element_type=F32).astype(BF16)
    q = projected[:, :WIDTH] * jnp.asarray(HD**-0.5, BF16)
    own_k = projected[:, WIDTH : 2 * WIDTH]
    own_v = projected[:, 2 * WIDTH :]
    q_ref[...] = q

    targets = [owner_s[branch_s[r]] for r in range(requests)]
    for r in range(requests):
        count_s[targets[r]] = 0
    places = []
    for r in range(requests):
        earlier = count_s[targets[r]]
        count_s[targets[r]] = earlier + 1
        places.append(targets[r] * CAPACITY + earlier)

    slots = out_ref.shape[0]
    column = iota((8, rows), 1)
    lane_pos = jnp.zeros((8, rows), jnp.int32)
    for r in range(requests):
        lane_pos = jnp.where((column >> 2) == r, places[r] * DRAFTS, lane_pos)
    lane_pos = lane_pos + (column & 3)
    select = iota((slots, rows), 0) == jnp.broadcast_to(lane_pos[:1], (slots, rows))
    out_ref[...] = jnp.dot(
        jnp.where(select, 1.0, 0.0).astype(BF16), q, preferred_element_type=F32
    ).astype(BF16)

    row = iota((rows, WIDTH), 0)
    owner_row = jnp.zeros((rows, WIDTH), jnp.int32)
    leaf_row = jnp.zeros((rows, WIDTH), jnp.int32)
    new_row = jnp.zeros((rows, WIDTH), jnp.int32)
    for r in range(requests):
        mine = (row >> 2) == r
        owner_row = jnp.where(mine, places[r], owner_row)
        leaf_row = jnp.where(mine, leaf_len_s[r], leaf_row)
        new_row = jnp.where(mine, new_s[r], new_row)
    pos_ref[...] = (owner_row >> 1) * 16 + (owner_row & 1) * 4 + (row & 3)
    use_ref[...] = jnp.where((row & 3) < new_row, 1.0, 0.0)

    stacked = stack_heads(q)
    leaf_two = jnp.concatenate([leaf_row, leaf_row], axis=0)
    new_two = jnp.concatenate([new_row, new_row], axis=0)
    both = 2 * rows
    span = leaf_k_ref.shape[0]
    score_leaf = dot_nt(stacked, leaf_k_ref[...])
    score_own = dot_nt(stacked, own_k)
    key = iota((both, span), 1)
    request_of = (iota((both, span), 0) & (rows - 1)) >> 2
    leaf_wide = jnp.concatenate([leaf_two] * (span // WIDTH), axis=1)
    ok_leaf = ((key >> 4) == request_of) & ((key & 15) < leaf_wide)
    key = iota((both, rows), 1)
    query = iota((both, rows), 0) & (rows - 1)
    ok_own = (
        ((key >> 2) == (query >> 2))
        & ((key & 3) <= (query & 3))
        & ((key & 3) < new_two[:, :rows])
    )
    score_leaf = jnp.where(ok_leaf, score_leaf, NEG)
    score_own = jnp.where(ok_own, score_own, NEG)
    peak = jnp.maximum(
        jnp.max(score_leaf, axis=1, keepdims=True), jnp.max(score_own, axis=1, keepdims=True)
    )
    w_leaf = jnp.where(ok_leaf, jnp.exp(score_leaf - peak), 0.0)
    w_own = jnp.where(ok_own, jnp.exp(score_own - peak), 0.0)
    total = jnp.sum(w_leaf, axis=1, keepdims=True) + jnp.sum(w_own, axis=1, keepdims=True)
    weighted = jnp.dot(
        w_leaf.astype(BF16), leaf_v_ref[...], preferred_element_type=F32
    ) + jnp.dot(w_own.astype(BF16), own_v, preferred_element_type=F32)
    m_ref[...] = merge_heads(jnp.broadcast_to(peak, (both, WIDTH)))
    t_ref[...] = merge_heads(jnp.broadcast_to(total, (both, WIDTH)))
    o_ref[...] = merge_heads(weighted)


def branch_kernel(len_s, q_ref, k_ref, v_ref, out_ref):
    count = q_ref.shape[0]
    span = k_ref.shape[0]
    block = 128
    valid = iota((2 * block, span), 1) < len_s[0]
    lane = iota((block, WIDTH), 1) & (HD - 1)
    for b in range(count // block):
        stacked = stack_heads(q_ref[b * block : (b + 1) * block])
        score = jnp.where(valid, dot_nt(stacked, k_ref[...]), NEG)
        peak = jnp.max(score, axis=1, keepdims=True)
        weights = jnp.exp(score - peak)
        total = jnp.sum(weights, axis=1, keepdims=True)
        weighted = jnp.dot(weights.astype(BF16), v_ref[...], preferred_element_type=F32)
        part = merge_heads(weighted / total)
        level = merge_heads(jnp.broadcast_to(peak + jnp.log(total), (2 * block, WIDTH)))
        one = level.astype(BF16).astype(F32)
        two = (level - one).astype(BF16).astype(F32)
        three = level - one - two
        pieces = jnp.where(
            lane == 0, one, jnp.where(lane == 1, two, jnp.where(lane == 2, three, 0.0))
        )
        packed = jnp.concatenate(
            [part.reshape(block // 8, 8, WIDTH), pieces.reshape(block // 8, 8, WIDTH)], axis=1
        )
        out_ref[2 * b * block : 2 * (b + 1) * block] = packed.reshape(2 * block, WIDTH).astype(BF16)


def root_kernel(q_ref, m_ref, t_ref, o_ref, *refs):
    pieces, (mo_ref, to_ref, oo_ref, score_ref) = refs[:-4], refs[-4:]
    rows = q_ref.shape[0]
    both = 2 * rows
    stacked = stack_heads(q_ref[...])
    chunk = 1024
    spans = [(ref, s) for ref in pieces for s in range(0, ref.shape[0], chunk)]

    def half(ref, start, second):
        data = ref[start : start + chunk].reshape(chunk // 128, 128, WIDTH)
        return data[:, 64 * second : 64 * second + 64].reshape(chunk // 2, WIDTH)

    top = jnp.full((both, WIDTH), NEG, F32)
    for n, (ref, start) in enumerate(spans):
        score = dot_nt(stacked, half(ref, start, 0))
        score_ref[:, n * (chunk // 2) : (n + 1) * (chunk // 2)] = score
        for s in range(0, chunk // 2, WIDTH):
            top = jnp.maximum(top, score[:, s : s + WIDTH])
    peak = jnp.max(top, axis=1, keepdims=True)
    total = jnp.zeros((both, WIDTH), F32)
    weighted = jnp.zeros((both, WIDTH), F32)
    for n, (ref, start) in enumerate(spans):
        weights = jnp.exp(score_ref[:, n * (chunk // 2) : (n + 1) * (chunk // 2)] - peak)
        for s in range(0, chunk // 2, WIDTH):
            total = total + weights[:, s : s + WIDTH]
        weighted = weighted + jnp.dot(
            weights.astype(BF16), half(ref, start, 1), preferred_element_type=F32
        )
    total = jnp.sum(total, axis=1, keepdims=True)
    root_m = merge_heads(jnp.broadcast_to(peak, (both, WIDTH)))
    root_t = merge_heads(jnp.broadcast_to(total, (both, WIDTH)))
    root_o = merge_heads(weighted)
    local_m = m_ref[...]
    high = jnp.maximum(root_m, local_m)
    scale_root = jnp.exp(root_m - high)
    scale_local = jnp.exp(local_m - high)
    mo_ref[...] = high
    to_ref[...] = root_t * scale_root + t_ref[...] * scale_local
    oo_ref[...] = root_o * scale_root + o_ref[...] * scale_local


def finish_kernel(back_ref, pos_ref, use_ref, m_ref, t_ref, o_ref, w_ref, out_ref):
    rows = pos_ref.shape[0]
    span = back_ref.shape[0]
    pos = pos_ref[...]
    lane = iota((rows, WIDTH), 1)
    part_pick = jnp.concatenate(
        [jnp.where(lane + s == pos, 1.0, 0.0) for s in range(0, span, WIDTH)], axis=1
    ).astype(BF16)
    level_pick = jnp.concatenate(
        [jnp.where(lane + s == pos + 8, 1.0, 0.0) for s in range(0, span, WIDTH)], axis=1
    ).astype(BF16)
    picked = jnp.dot(
        jnp.concatenate([part_pick, level_pick], axis=0),
        back_ref[...],
        preferred_element_type=F32,
    )
    part = picked[:rows]
    same = (iota((WIDTH, WIDTH), 0) < HD) == (iota((WIDTH, WIDTH), 1) < HD)
    level = jnp.dot(
        picked[rows:].astype(BF16),
        jnp.where(same, 1.0, 0.0).astype(BF16),
        preferred_element_type=F32,
    )
    high = jnp.maximum(m_ref[...], level)
    scale_rest = jnp.exp(m_ref[...] - high)
    scale_branch = jnp.exp(level - high)
    attention = (o_ref[...] * scale_rest + part * scale_branch) / (
        t_ref[...] * scale_rest + scale_branch
    )
    attention = jnp.where(use_ref[...] > 0.5, attention, 0.0).astype(BF16)
    terms = jnp.dot(attention, w_ref[...], preferred_element_type=F32).astype(BF16)
    for s in range(w_ref.shape[1] // WIDTH):
        out_ref[s * rows : (s + 1) * rows] = terms[:, s * WIDTH : (s + 1) * WIDTH]


def add_kernel(in_ref, out_ref):
    rows = out_ref.shape[0]
    total = in_ref[:rows].astype(F32)
    for s in range(1, in_ref.shape[0] // rows):
        total = total + in_ref[s * rows : (s + 1) * rows].astype(F32)
    out_ref[...] = total.astype(BF16)


def sds(rows, dtype):
    return jax.ShapeDtypeStruct((rows, WIDTH), dtype)


def local(
    tokens,
    norm_gain,
    w_qkv,
    w_out,
    root_kv,
    branch_kv,
    leaf_kv,
    branch,
    node_owner,
    branch_len,
    leaf_len,
    new_count,
):
    rows = tokens.shape[0]
    nodes = node_owner.shape[0]
    tensor = w_out.shape[1] // WIDTH
    planes = lax.axis_size("z")

    root = jnp.concatenate([root_kv[:, 0], root_kv[:, 1]], axis=0)
    along_z = lax.all_to_all(
        jnp.broadcast_to(root[None], (planes,) + root.shape).reshape(-1, WIDTH), "z", 0, 0, tiled=True
    )
    near = lax.ppermute(along_z, "x", [(i, i ^ 1) for i in range(4)])
    pair = jnp.concatenate([along_z, near], axis=0)
    far = lax.ppermute(pair, "x", [(i, i ^ 2) for i in range(4)])
    mine = jnp.concatenate([pair, far], axis=0)
    other = lax.ppermute(mine, "c", [(0, 1), (1, 0)])

    q, outgoing, m_local, t_local, o_local, pos, use = pl.pallas_call(
        front_kernel,
        out_shape=[
            sds(rows, BF16),
            sds(nodes * CAPACITY * DRAFTS, BF16),
            sds(rows, F32),
            sds(rows, F32),
            sds(rows, F32),
            sds(rows, jnp.int32),
            sds(rows, F32),
        ],
        in_specs=[SM] * 4 + [VM] * 5,
        out_specs=[VM] * 7,
        scratch_shapes=[pltpu.SMEM((nodes,), jnp.int32)],
        compiler_params=PARAMS,
        name="front",
    )(
        branch[:, 0],
        node_owner,
        leaf_len,
        new_count,
        tokens,
        norm_gain[None],
        w_qkv.reshape(w_qkv.shape[0], -1),
        leaf_kv[:, :, 0].reshape(-1, WIDTH),
        leaf_kv[:, :, 1].reshape(-1, WIDTH),
    )

    incoming = lax.all_to_all(outgoing, REQ, 0, 0, tiled=True)
    me = lax.axis_index(REQ)
    owned = jnp.sum(jnp.where(node_owner == me, branch_len, 0)).reshape(1)
    answer = pl.pallas_call(
        branch_kernel,
        out_shape=sds(2 * incoming.shape[0], BF16),
        in_specs=[SM, VM, VM, VM],
        out_specs=VM,
        compiler_params=PARAMS,
        name="branch",
    )(owned, incoming, branch_kv[0, :, 0], branch_kv[0, :, 1])
    back = lax.all_to_all(answer, REQ, 0, 0, tiled=True)

    pieces = (mine, other)
    keys = sum(p.shape[0] for p in pieces) // 2
    m_rest, t_rest, o_rest = pl.pallas_call(
        root_kernel,
        out_shape=[sds(rows, F32)] * 3,
        in_specs=[VM] * (4 + len(pieces)),
        out_specs=[VM] * 3,
        scratch_shapes=[pltpu.VMEM((2 * rows, keys), F32)],
        compiler_params=PARAMS,
        name="root",
    )(q, m_local, t_local, o_local, *pieces)

    terms = pl.pallas_call(
        finish_kernel,
        out_shape=sds(tensor * rows, BF16),
        in_specs=[VM] * 7,
        out_specs=VM,
        compiler_params=PARAMS,
        name="finish",
    )(back, pos, use, m_rest, t_rest, o_rest, w_out)
    shares = lax.all_to_all(terms, "y", 0, 0, tiled=True)
    return pl.pallas_call(
        add_kernel,
        out_shape=sds(rows, BF16),
        in_specs=[VM],
        out_specs=VM,
        compiler_params=PARAMS,
        name="add",
    )(shares)


def solution(mesh):
    split = Mesh(mesh.devices.reshape(8, 4, 2, 8), REQ + ("y",))
    placed = (
        P(REQ, None),
        P(),
        P(None, None, "y"),
        P("y", None),
        P(REQ, None, "y"),
        P(REQ, None, None, "y"),
        P(REQ, None, None, "y"),
        P(REQ, None),
        P(),
        P(),
        P(REQ),
        P(REQ),
    )
    return jax.shard_map(
        local, mesh=split, in_specs=placed, out_specs=P(REQ, "y"), check_vma=False
    )
```

```python
import jax
import jax.numpy as jnp
from jax import lax
from jax.experimental import pallas as pl
from jax.experimental.pallas import tpu as pltpu
from jax.sharding import Mesh
from jax.sharding import PartitionSpec as P

HD = 64
WIDTH = 128
DRAFTS = 4
CAPACITY = 2
NEG = -1e30
F32 = jnp.float32
BF16 = jnp.bfloat16
REQ = ("z", "x", "c")
VM = pl.BlockSpec(memory_space=pltpu.VMEM)
SM = pl.BlockSpec(memory_space=pltpu.SMEM)
PARAMS = pltpu.CompilerParams(vmem_limit_bytes=48 * 1024 * 1024)


def iota(shape, dim):
    return lax.broadcasted_iota(jnp.int32, shape, dim)


def low_lanes(shape):
    return iota(shape, len(shape) - 1) < HD


def stack_heads(q):
    low = low_lanes(q.shape)
    zero = jnp.zeros_like(q)
    return jnp.concatenate([jnp.where(low, q, zero), jnp.where(low, zero, q)], axis=0)


def merge_heads(x):
    n = x.shape[0] // 2
    return jnp.where(low_lanes((n, WIDTH)), x[:n], x[n:])


def dot_nt(a, b):
    return lax.dot_general(a, b, (((1,), (1,)), ((), ())), preferred_element_type=F32)


def front_kernel(
    branch_s,
    owner_s,
    leaf_len_s,
    new_s,
    tok_ref,
    gain_ref,
    w_ref,
    leaf_k_ref,
    leaf_v_ref,
    q_ref,
    out_ref,
    m_ref,
    t_ref,
    o_ref,
    pos_ref,
    use_ref,
    count_s,
):
    rows = tok_ref.shape[0]
    requests = rows // DRAFTS
    x = tok_ref[...].astype(F32)
    scale = lax.rsqrt(jnp.mean(x * x, axis=1, keepdims=True) + 1e-05)
    normed = (x * scale * gain_ref[...]).astype(BF16)
    projected = jnp.dot(normed, w_ref[...], preferred_element_type=F32).astype(BF16)
    q = projected[:, :WIDTH] * jnp.asarray(HD**-0.5, BF16)
    own_k = projected[:, WIDTH : 2 * WIDTH]
    own_v = projected[:, 2 * WIDTH :]
    q_ref[...] = q

    targets = [owner_s[branch_s[r]] for r in range(requests)]
    for r in range(requests):
        count_s[targets[r]] = 0
    places = []
    for r in range(requests):
        earlier = count_s[targets[r]]
        count_s[targets[r]] = earlier + 1
        places.append(targets[r] * CAPACITY + earlier)

    slots = out_ref.shape[0]
    column = iota((8, rows), 1)
    lane_pos = jnp.zeros((8, rows), jnp.int32)
    for r in range(requests):
        lane_pos = jnp.where((column >> 2) == r, places[r] * DRAFTS, lane_pos)
    lane_pos = lane_pos + (column & 3)
    select = iota((slots, rows), 0) == jnp.broadcast_to(lane_pos[:1], (slots, rows))
    out_ref[...] = jnp.dot(
        jnp.where(select, 1.0, 0.0).astype(BF16), q, preferred_element_type=F32
    ).astype(BF16)

    row = iota((rows, WIDTH), 0)
    owner_row = jnp.zeros((rows, WIDTH), jnp.int32)
    leaf_row = jnp.zeros((rows, WIDTH), jnp.int32)
    new_row = jnp.zeros((rows, WIDTH), jnp.int32)
    for r in range(requests):
        mine = (row >> 2) == r
        owner_row = jnp.where(mine, places[r], owner_row)
        leaf_row = jnp.where(mine, leaf_len_s[r], leaf_row)
        new_row = jnp.where(mine, new_s[r], new_row)
    pos_ref[...] = (owner_row >> 1) * 16 + (owner_row & 1) * 4 + (row & 3)
    use_ref[...] = jnp.where((row & 3) < new_row, 1.0, 0.0)

    stacked = stack_heads(q)
    leaf_two = jnp.concatenate([leaf_row, leaf_row], axis=0)
    new_two = jnp.concatenate([new_row, new_row], axis=0)
    both = 2 * rows
    span = leaf_k_ref.shape[0]
    score_leaf = dot_nt(stacked, leaf_k_ref[...])
    score_own = dot_nt(stacked, own_k)
    key = iota((both, span), 1)
    request_of = (iota((both, span), 0) & (rows - 1)) >> 2
    leaf_wide = jnp.concatenate([leaf_two] * (span // WIDTH), axis=1)
    ok_leaf = ((key >> 4) == request_of) & ((key & 15) < leaf_wide)
    key = iota((both, rows), 1)
    query = iota((both, rows), 0) & (rows - 1)
    ok_own = (
        ((key >> 2) == (query >> 2))
        & ((key & 3) <= (query & 3))
        & ((key & 3) < new_two[:, :rows])
    )
    score_leaf = jnp.where(ok_leaf, score_leaf, NEG)
    score_own = jnp.where(ok_own, score_own, NEG)
    peak = jnp.maximum(
        jnp.max(score_leaf, axis=1, keepdims=True), jnp.max(score_own, axis=1, keepdims=True)
    )
    w_leaf = jnp.where(ok_leaf, jnp.exp(score_leaf - peak), 0.0)
    w_own = jnp.where(ok_own, jnp.exp(score_own - peak), 0.0)
    total = jnp.sum(w_leaf, axis=1, keepdims=True) + jnp.sum(w_own, axis=1, keepdims=True)
    weighted = jnp.dot(
        w_leaf.astype(BF16), leaf_v_ref[...], preferred_element_type=F32
    ) + jnp.dot(w_own.astype(BF16), own_v, preferred_element_type=F32)
    m_ref[...] = merge_heads(jnp.broadcast_to(peak, (both, WIDTH)))
    t_ref[...] = merge_heads(jnp.broadcast_to(total, (both, WIDTH)))
    o_ref[...] = merge_heads(weighted)


def branch_kernel(len_s, q_ref, k_ref, v_ref, out_ref):
    count = q_ref.shape[0]
    span = k_ref.shape[0]
    block = 128
    valid = iota((2 * block, span), 1) < len_s[0]
    lane = iota((block, WIDTH), 1) & (HD - 1)
    for b in range(count // block):
        stacked = stack_heads(q_ref[b * block : (b + 1) * block])
        score = jnp.where(valid, dot_nt(stacked, k_ref[...]), NEG)
        peak = jnp.max(score, axis=1, keepdims=True)
        weights = jnp.exp(score - peak)
        total = jnp.sum(weights, axis=1, keepdims=True)
        weighted = jnp.dot(weights.astype(BF16), v_ref[...], preferred_element_type=F32)
        part = merge_heads(weighted / total)
        level = merge_heads(jnp.broadcast_to(peak + jnp.log(total), (2 * block, WIDTH)))
        one = level.astype(BF16).astype(F32)
        two = (level - one).astype(BF16).astype(F32)
        three = level - one - two
        pieces = jnp.where(
            lane == 0, one, jnp.where(lane == 1, two, jnp.where(lane == 2, three, 0.0))
        )
        packed = jnp.concatenate(
            [part.reshape(block // 8, 8, WIDTH), pieces.reshape(block // 8, 8, WIDTH)], axis=1
        )
        out_ref[2 * b * block : 2 * (b + 1) * block] = packed.reshape(2 * block, WIDTH).astype(BF16)


def root_kernel(q_ref, peer_ref, m_ref, t_ref, o_ref, *refs):
    pieces, (mo_ref, to_ref, oo_ref, send_ref, score_ref) = refs[:-5], refs[-5:]
    rows = q_ref.shape[0]
    both = 4 * rows
    stacked = jnp.concatenate([stack_heads(q_ref[...]), stack_heads(peer_ref[...])], axis=0)
    chunk = 1024
    spans = [(ref, s) for ref in pieces for s in range(0, ref.shape[0], chunk)]

    def half(ref, start, second):
        data = ref[start : start + chunk].reshape(chunk // 128, 128, WIDTH)
        return data[:, 64 * second : 64 * second + 64].reshape(chunk // 2, WIDTH)

    top = jnp.full((both, WIDTH), NEG, F32)
    for n, (ref, start) in enumerate(spans):
        score = dot_nt(stacked, half(ref, start, 0))
        score_ref[:, n * (chunk // 2) : (n + 1) * (chunk // 2)] = score
        for s in range(0, chunk // 2, WIDTH):
            top = jnp.maximum(top, score[:, s : s + WIDTH])
    peak = jnp.max(top, axis=1, keepdims=True)
    total = jnp.zeros((both, WIDTH), F32)
    weighted = jnp.zeros((both, WIDTH), F32)
    for n, (ref, start) in enumerate(spans):
        weights = jnp.exp(score_ref[:, n * (chunk // 2) : (n + 1) * (chunk // 2)] - peak)
        for s in range(0, chunk // 2, WIDTH):
            total = total + weights[:, s : s + WIDTH]
        weighted = weighted + jnp.dot(
            weights.astype(BF16), half(ref, start, 1), preferred_element_type=F32
        )
    total = jnp.sum(total, axis=1, keepdims=True)
    peak = jnp.broadcast_to(peak, (both, WIDTH))
    total = jnp.broadcast_to(total, (both, WIDTH))
    root_m = merge_heads(peak[: both // 2])
    root_t = merge_heads(total[: both // 2])
    root_o = merge_heads(weighted[: both // 2])
    local_m = m_ref[...]
    high = jnp.maximum(root_m, local_m)
    scale_root = jnp.exp(root_m - high)
    scale_local = jnp.exp(local_m - high)
    mo_ref[...] = high
    to_ref[...] = root_t * scale_root + t_ref[...] * scale_local
    oo_ref[...] = root_o * scale_root + o_ref[...] * scale_local
    peer_t = merge_heads(total[both // 2 :])
    send_ref[:rows] = merge_heads(weighted[both // 2 :]) / peer_t
    send_ref[rows:] = merge_heads(peak[both // 2 :]) + jnp.log(peer_t)


def finish_kernel(back_ref, peer_ref, pos_ref, use_ref, m_ref, t_ref, o_ref, w_ref, out_ref):
    rows = pos_ref.shape[0]
    span = back_ref.shape[0]
    pos = pos_ref[...]
    lane = iota((rows, WIDTH), 1)
    part_pick = jnp.concatenate(
        [jnp.where(lane + s == pos, 1.0, 0.0) for s in range(0, span, WIDTH)], axis=1
    ).astype(BF16)
    level_pick = jnp.concatenate(
        [jnp.where(lane + s == pos + 8, 1.0, 0.0) for s in range(0, span, WIDTH)], axis=1
    ).astype(BF16)
    picked = jnp.dot(
        jnp.concatenate([part_pick, level_pick], axis=0),
        back_ref[...],
        preferred_element_type=F32,
    )
    part = picked[:rows]
    same = (iota((WIDTH, WIDTH), 0) < HD) == (iota((WIDTH, WIDTH), 1) < HD)
    level = jnp.dot(
        picked[rows:].astype(BF16),
        jnp.where(same, 1.0, 0.0).astype(BF16),
        preferred_element_type=F32,
    )
    peer = peer_ref[rows:]
    high = jnp.maximum(jnp.maximum(m_ref[...], level), peer)
    scale_rest = jnp.exp(m_ref[...] - high)
    scale_peer = jnp.exp(peer - high)
    scale_branch = jnp.exp(level - high)
    attention = (
        o_ref[...] * scale_rest + peer_ref[:rows] * scale_peer + part * scale_branch
    ) / (t_ref[...] * scale_rest + scale_peer + scale_branch)
    attention = jnp.where(use_ref[...] > 0.5, attention, 0.0).astype(BF16)
    terms = jnp.dot(attention, w_ref[...], preferred_element_type=F32).astype(BF16)
    for s in range(w_ref.shape[1] // WIDTH):
        out_ref[s * rows : (s + 1) * rows] = terms[:, s * WIDTH : (s + 1) * WIDTH]


def add_kernel(in_ref, out_ref):
    rows = out_ref.shape[0]
    total = in_ref[:rows].astype(F32)
    for s in range(1, in_ref.shape[0] // rows):
        total = total + in_ref[s * rows : (s + 1) * rows].astype(F32)
    out_ref[...] = total.astype(BF16)


def sds(rows, dtype):
    return jax.ShapeDtypeStruct((rows, WIDTH), dtype)


def local(
    tokens,
    norm_gain,
    w_qkv,
    w_out,
    root_kv,
    branch_kv,
    leaf_kv,
    branch,
    node_owner,
    branch_len,
    leaf_len,
    new_count,
):
    rows = tokens.shape[0]
    nodes = node_owner.shape[0]
    tensor = w_out.shape[1] // WIDTH
    planes = lax.axis_size("z")

    root = jnp.concatenate([root_kv[:, 0], root_kv[:, 1]], axis=0)
    along_z = lax.all_to_all(
        jnp.broadcast_to(root[None], (planes,) + root.shape).reshape(-1, WIDTH), "z", 0, 0, tiled=True
    )
    q, outgoing, m_local, t_local, o_local, pos, use = pl.pallas_call(
        front_kernel,
        out_shape=[
            sds(rows, BF16),
            sds(nodes * CAPACITY * DRAFTS, BF16),
            sds(rows, F32),
            sds(rows, F32),
            sds(rows, F32),
            sds(rows, jnp.int32),
            sds(rows, F32),
        ],
        in_specs=[SM] * 4 + [VM] * 5,
        out_specs=[VM] * 7,
        scratch_shapes=[pltpu.SMEM((nodes,), jnp.int32)],
        compiler_params=PARAMS,
        name="front",
    )(
        branch[:, 0],
        node_owner,
        leaf_len,
        new_count,
        tokens,
        norm_gain[None],
        w_qkv.reshape(w_qkv.shape[0], -1),
        leaf_kv[:, :, 0].reshape(-1, WIDTH),
        leaf_kv[:, :, 1].reshape(-1, WIDTH),
    )

    q_peer = lax.ppermute(q, "c", [(0, 1), (1, 0)])
    along_z, outgoing, q_peer = lax.optimization_barrier((along_z, outgoing, q_peer))
    near = lax.ppermute(along_z, "x", [(i, i ^ 1) for i in range(4)])
    pair = jnp.concatenate([along_z, near], axis=0)
    far = lax.ppermute(pair, "x", [(i, i ^ 2) for i in range(4)])
    incoming = lax.all_to_all(outgoing, REQ, 0, 0, tiled=True)
    me = lax.axis_index(REQ)
    owned = jnp.sum(jnp.where(node_owner == me, branch_len, 0)).reshape(1)
    answer = pl.pallas_call(
        branch_kernel,
        out_shape=sds(2 * incoming.shape[0], BF16),
        in_specs=[SM, VM, VM, VM],
        out_specs=VM,
        compiler_params=PARAMS,
        name="branch",
        cost_estimate=pl.CostEstimate(flops=5000000000, transcendentals=0, bytes_accessed=0),
    )(owned, incoming, branch_kv[0, :, 0], branch_kv[0, :, 1])
    _, far = lax.optimization_barrier((answer, far))
    back = lax.all_to_all(answer, REQ, 0, 0, tiled=True)

    keys = (pair.shape[0] + far.shape[0]) // 2
    m_rest, t_rest, o_rest, send = pl.pallas_call(
        root_kernel,
        out_shape=[sds(rows, F32)] * 3 + [sds(2 * rows, F32)],
        in_specs=[VM] * 7,
        out_specs=[VM] * 4,
        scratch_shapes=[pltpu.VMEM((4 * rows, keys), F32)],
        compiler_params=PARAMS,
        name="root",
    )(q, q_peer, m_local, t_local, o_local, pair, far)
    peer = lax.ppermute(send, "c", [(0, 1), (1, 0)])

    terms = pl.pallas_call(
        finish_kernel,
        out_shape=sds(tensor * rows, BF16),
        in_specs=[VM] * 8,
        out_specs=VM,
        compiler_params=PARAMS,
        name="finish",
    )(back, peer, pos, use, m_rest, t_rest, o_rest, w_out)
    shares = lax.all_to_all(terms, "y", 0, 0, tiled=True)
    return pl.pallas_call(
        add_kernel,
        out_shape=sds(rows, BF16),
        in_specs=[VM],
        out_specs=VM,
        compiler_params=PARAMS,
        name="add",
    )(shares)


def solution(mesh):
    split = Mesh(mesh.devices.reshape(8, 4, 2, 8), REQ + ("y",))
    placed = (
        P(REQ, None),
        P(),
        P(None, None, "y"),
        P("y", None),
        P(REQ, None, "y"),
        P(REQ, None, None, "y"),
        P(REQ, None, None, "y"),
        P(REQ, None),
        P(),
        P(),
        P(REQ),
        P(REQ),
    )
    return jax.shard_map(
        local, mesh=split, in_specs=placed, out_specs=P(REQ, "y"), check_vma=False
    )
```

```python
import jax
import jax.numpy as jnp
from jax import lax
from jax.experimental import pallas as pl
from jax.experimental.pallas import tpu as pltpu
from jax.sharding import Mesh
from jax.sharding import PartitionSpec as P

HD = 64
WIDTH = 128
DRAFTS = 4
CAPACITY = 2
PACKET = 10
NEG = -1e30
F32 = jnp.float32
BF16 = jnp.bfloat16
REQ = ("z", "x", "c")
VM = pl.BlockSpec(memory_space=pltpu.VMEM)
SM = pl.BlockSpec(memory_space=pltpu.SMEM)
PARAMS = pltpu.CompilerParams(vmem_limit_bytes=48 * 1024 * 1024)


def iota(shape, dim):
    return lax.broadcasted_iota(jnp.int32, shape, dim)


def low_lanes(shape):
    return iota(shape, len(shape) - 1) < HD


def stack_heads(q):
    low = low_lanes(q.shape)
    zero = jnp.zeros_like(q)
    return jnp.concatenate([jnp.where(low, q, zero), jnp.where(low, zero, q)], axis=0)


def merge_heads(x):
    n = x.shape[0] // 2
    return jnp.where(low_lanes((n, WIDTH)), x[:n], x[n:])


def dot_nt(a, b):
    return lax.dot_general(a, b, (((1,), (1,)), ((), ())), preferred_element_type=F32)


def pack_kernel(in_ref, out_ref):
    data = in_ref[...].astype(F32)
    both = jnp.concatenate([data[:, 0], data[:, 1]], axis=0).astype(BF16)
    size = both.shape[0]
    for s in range(out_ref.shape[0] // size):
        out_ref[s * size : (s + 1) * size] = both


def places_of(branch_s, owner_s, count_s, requests):
    targets = [owner_s[branch_s[r]] for r in range(requests)]
    for r in range(requests):
        count_s[targets[r]] = 0
    places = []
    for r in range(requests):
        earlier = count_s[targets[r]]
        count_s[targets[r]] = earlier + 1
        places.append(targets[r] * CAPACITY + earlier)
    return places


def local_group(q, own_k, own_v, leaf_k, leaf_v, leaf_row, new_row):
    rows = q.shape[0]
    stacked = stack_heads(q)
    leaf_two = jnp.concatenate([leaf_row, leaf_row], axis=0)
    new_two = jnp.concatenate([new_row, new_row], axis=0)
    both = 2 * rows
    span = leaf_k.shape[0]
    score_leaf = dot_nt(stacked, leaf_k)
    score_own = dot_nt(stacked, own_k)
    key = iota((both, span), 1)
    request_of = (iota((both, span), 0) & (rows - 1)) >> 2
    leaf_wide = jnp.concatenate([leaf_two] * (span // WIDTH), axis=1)
    ok_leaf = ((key >> 4) == request_of) & ((key & 15) < leaf_wide)
    key = iota((both, rows), 1)
    query = iota((both, rows), 0) & (rows - 1)
    ok_own = (
        ((key >> 2) == (query >> 2))
        & ((key & 3) <= (query & 3))
        & ((key & 3) < new_two[:, :rows])
    )
    score_leaf = jnp.where(ok_leaf, score_leaf, NEG)
    score_own = jnp.where(ok_own, score_own, NEG)
    peak = jnp.maximum(
        jnp.max(score_leaf, axis=1, keepdims=True), jnp.max(score_own, axis=1, keepdims=True)
    )
    w_leaf = jnp.where(ok_leaf, jnp.exp(score_leaf - peak), 0.0)
    w_own = jnp.where(ok_own, jnp.exp(score_own - peak), 0.0)
    total = jnp.sum(w_leaf, axis=1, keepdims=True) + jnp.sum(w_own, axis=1, keepdims=True)
    weighted = jnp.dot(w_leaf.astype(BF16), leaf_v, preferred_element_type=F32) + jnp.dot(
        w_own.astype(BF16), own_v, preferred_element_type=F32
    )
    return (
        merge_heads(jnp.broadcast_to(peak, (both, WIDTH))),
        merge_heads(jnp.broadcast_to(total, (both, WIDTH))),
        merge_heads(weighted),
    )


def front_kernel(
    branch_s,
    owner_s,
    leaf_len_s,
    new_s,
    tok_hbm,
    gain_ref,
    w_ref,
    leaf_k_ref,
    leaf_v_ref,
    q_ref,
    out_ref,
    m_ref,
    t_ref,
    o_ref,
    pos_ref,
    use_ref,
    tok_ref,
    count_s,
    sem,
):
    rows = tok_ref.shape[0]
    requests = rows // DRAFTS
    fetch = pltpu.make_async_copy(tok_hbm, tok_ref, sem)
    fetch.start()
    places = places_of(branch_s, owner_s, count_s, requests)
    slots = out_ref.shape[0]
    column = iota((8, rows), 1)
    lane_pos = jnp.zeros((8, rows), jnp.int32)
    for r in range(requests):
        lane_pos = jnp.where((column >> 2) == r, places[r] * DRAFTS, lane_pos)
    lane_pos = lane_pos + (column & 3)
    select = iota((slots, rows), 0) == jnp.broadcast_to(lane_pos[:1], (slots, rows))
    select = jnp.where(select, 1.0, 0.0).astype(BF16)
    row = iota((rows, WIDTH), 0)
    place_row = jnp.zeros((rows, WIDTH), jnp.int32)
    leaf_row = jnp.zeros((rows, WIDTH), jnp.int32)
    new_row = jnp.zeros((rows, WIDTH), jnp.int32)
    for r in range(requests):
        mine = (row >> 2) == r
        place_row = jnp.where(mine, places[r], place_row)
        leaf_row = jnp.where(mine, leaf_len_s[r], leaf_row)
        new_row = jnp.where(mine, new_s[r], new_row)
    pos_ref[...] = place_row * DRAFTS + (row & 3)
    use_ref[...] = jnp.where((row & 3) < new_row, 1.0, 0.0)
    fetch.wait()

    x = tok_ref[...].astype(F32)
    scale = lax.rsqrt(jnp.mean(x * x, axis=1, keepdims=True) + 1e-05)
    normed = (x * scale * gain_ref[...]).astype(BF16)

    def project(n):
        return jnp.dot(normed, w_ref[n], preferred_element_type=F32).astype(BF16)

    q = project(0) * jnp.asarray(HD**-0.5, BF16)
    q_ref[...] = q
    out_ref[...] = jnp.dot(select, q, preferred_element_type=F32).astype(BF16)
    m_ref[...], t_ref[...], o_ref[...] = local_group(
        q, project(1), project(2), leaf_k_ref[...], leaf_v_ref[...], leaf_row, new_row
    )


def branch_kernel(len_s, q_ref, k_ref, v_ref, out_ref):
    count = q_ref.shape[0]
    span = k_ref.shape[0]
    block = 128
    packets = block // 8
    valid = iota((2 * block, span), 1) < len_s[0]
    lane = iota((block, WIDTH), 1)
    mine = (lane >> 4) == (iota((block, WIDTH), 0) & 7)
    second = ((lane >> 3) & 1) == 1
    to = iota((packets * PACKET, block + packets), 0)
    frm = iota((packets * PACKET, block + packets), 1)
    goal = jnp.where(frm < block, (frm >> 3) * PACKET + (frm & 7), (frm - block) * PACKET + 8)
    spread = jnp.where(to == goal, 1.0, 0.0).astype(BF16)
    for b in range(count // block):
        stacked = stack_heads(q_ref[b * block : (b + 1) * block])
        score = jnp.where(valid, dot_nt(stacked, k_ref[...]), NEG)
        peak = jnp.max(score, axis=1, keepdims=True)
        weights = jnp.exp(score - peak)
        total = jnp.sum(weights, axis=1, keepdims=True)
        weighted = jnp.dot(weights.astype(BF16), v_ref[...], preferred_element_type=F32)
        part = merge_heads(weighted / total)
        level = jnp.broadcast_to(peak + jnp.log(total), (2 * block, WIDTH))
        level = jnp.where(second, level[block:], level[:block])
        one = level.astype(BF16).astype(F32)
        two = (level - one).astype(BF16).astype(F32)
        three = level - one - two
        term = lane & 7
        pieces = jnp.where(term == 0, one, jnp.where(term == 1, two, three))
        pieces = jnp.where(mine & (term < 3), pieces, 0.0)
        levels = jnp.sum(pieces.reshape(packets, 8, WIDTH), axis=1)
        packed = jnp.dot(
            spread,
            jnp.concatenate([part, levels], axis=0).astype(BF16),
            preferred_element_type=F32,
        )
        out_ref[b * packets * PACKET : (b + 1) * packets * PACKET] = packed.astype(BF16)


def root_kernel(q_ref, peer_ref, local_m_ref, local_t_ref, local_o_ref, *refs):
    pieces, (m_ref, t_ref, o_ref, send_ref, score_ref) = refs[:-5], refs[-5:]
    rows = q_ref.shape[0]
    both = 4 * rows
    stacked = jnp.concatenate([stack_heads(q_ref[...]), stack_heads(peer_ref[...])], axis=0)
    chunk = 1024
    spans = [(ref, s) for ref in pieces for s in range(0, ref.shape[0], chunk)]

    def half(ref, start, second):
        data = ref[start : start + chunk].reshape(chunk // 128, 128, WIDTH)
        return data[:, 64 * second : 64 * second + 64].reshape(chunk // 2, WIDTH)

    top = jnp.full((both, WIDTH), NEG, F32)
    for n, (ref, start) in enumerate(spans):
        score = dot_nt(stacked, half(ref, start, 0))
        score_ref[:, n * (chunk // 2) : (n + 1) * (chunk // 2)] = score
        for s in range(0, chunk // 2, WIDTH):
            top = jnp.maximum(top, score[:, s : s + WIDTH])
    peak = jnp.max(top, axis=1, keepdims=True)
    total = jnp.zeros((both, WIDTH), F32)
    weighted = jnp.zeros((both, WIDTH), F32)
    for n, (ref, start) in enumerate(spans):
        weights = jnp.exp(score_ref[:, n * (chunk // 2) : (n + 1) * (chunk // 2)] - peak)
        for s in range(0, chunk // 2, WIDTH):
            total = total + weights[:, s : s + WIDTH]
        weighted = weighted + jnp.dot(
            weights.astype(BF16), half(ref, start, 1), preferred_element_type=F32
        )
    total = jnp.sum(total, axis=1, keepdims=True)
    peak = jnp.broadcast_to(peak, (both, WIDTH))
    total = jnp.broadcast_to(total, (both, WIDTH))
    root_m = merge_heads(peak[: both // 2])
    root_t = merge_heads(total[: both // 2])
    root_o = merge_heads(weighted[: both // 2])
    local_m = local_m_ref[...]
    high = jnp.maximum(root_m, local_m)
    scale_root = jnp.exp(root_m - high)
    scale_local = jnp.exp(local_m - high)
    m_ref[...] = high
    t_ref[...] = root_t * scale_root + local_t_ref[...] * scale_local
    o_ref[...] = root_o * scale_root + local_o_ref[...] * scale_local
    peer_t = merge_heads(total[both // 2 :])
    send_ref[:rows] = merge_heads(weighted[both // 2 :]) / peer_t
    send_ref[rows:] = merge_heads(peak[both // 2 :]) + jnp.log(peer_t)


def finish_kernel(back_ref, peer_ref, pos_ref, use_ref, m_ref, t_ref, o_ref, w_ref, out_ref):
    rows = pos_ref.shape[0]
    span = back_ref.shape[0]
    pos = pos_ref[...]
    lane = iota((rows, WIDTH), 1)
    start = (pos >> 3) * PACKET
    query = pos & 7

    def pick(at):
        return jnp.concatenate(
            [jnp.where(lane + s == at, 1.0, 0.0) for s in range(0, span, WIDTH)], axis=1
        )

    picked = jnp.dot(
        jnp.concatenate([pick(start + query), pick(start + 8)], axis=0).astype(BF16),
        back_ref[...],
        preferred_element_type=F32,
    )
    part = picked[:rows]
    levels = jnp.where((lane >> 4) == query, picked[rows:], 0.0).astype(BF16)
    same = ((iota((WIDTH, WIDTH), 0) >> 3) & 1) == (iota((WIDTH, WIDTH), 1) >> 6)
    level = jnp.dot(levels, jnp.where(same, 1.0, 0.0).astype(BF16), preferred_element_type=F32)
    peer = peer_ref[rows:]
    high = jnp.maximum(jnp.maximum(m_ref[...], level), peer)
    scale_rest = jnp.exp(m_ref[...] - high)
    scale_peer = jnp.exp(peer - high)
    scale_branch = jnp.exp(level - high)
    attention = (
        o_ref[...] * scale_rest + peer_ref[:rows] * scale_peer + part * scale_branch
    ) / (t_ref[...] * scale_rest + scale_peer + scale_branch)
    attention = jnp.where(use_ref[...] > 0.5, attention, 0.0).astype(BF16)
    terms = jnp.dot(attention, w_ref[...], preferred_element_type=F32).astype(BF16)
    for s in range(w_ref.shape[1] // WIDTH):
        out_ref[s * rows : (s + 1) * rows] = terms[:, s * WIDTH : (s + 1) * WIDTH]


def add_kernel(in_ref, out_ref):
    rows = out_ref.shape[0]
    total = in_ref[:rows].astype(F32)
    for s in range(1, in_ref.shape[0] // rows):
        total = total + in_ref[s * rows : (s + 1) * rows].astype(F32)
    out_ref[...] = total.astype(BF16)


def sds(rows, dtype):
    return jax.ShapeDtypeStruct((rows, WIDTH), dtype)


def local(
    tokens,
    norm_gain,
    w_qkv,
    w_out,
    root_kv,
    branch_kv,
    leaf_kv,
    branch,
    node_owner,
    branch_len,
    leaf_len,
    new_count,
):
    rows = tokens.shape[0]
    nodes = node_owner.shape[0]
    tensor = w_out.shape[1] // WIDTH
    planes = lax.axis_size("z")

    packed = pl.pallas_call(
        pack_kernel,
        out_shape=sds(2 * root_kv.shape[0] * planes, BF16),
        in_specs=[VM],
        out_specs=VM,
        compiler_params=PARAMS,
        name="pack",
    )(root_kv)
    along_z = lax.all_to_all(packed, "z", 0, 0, tiled=True)
    q, outgoing, m_local, t_local, o_local, pos, use = pl.pallas_call(
        front_kernel,
        out_shape=[
            sds(rows, BF16),
            sds(nodes * CAPACITY * DRAFTS, BF16),
            sds(rows, F32),
            sds(rows, F32),
            sds(rows, F32),
            sds(rows, jnp.int32),
            sds(rows, F32),
        ],
        in_specs=[SM] * 4 + [pl.BlockSpec(memory_space=pltpu.HBM)] + [VM] * 4,
        out_specs=[VM] * 7,
        scratch_shapes=[
            pltpu.VMEM(tokens.shape, BF16),
            pltpu.SMEM((nodes,), jnp.int32),
            pltpu.SemaphoreType.DMA,
        ],
        compiler_params=PARAMS,
        name="front",
    )(
        branch[:, 0],
        node_owner,
        leaf_len,
        new_count,
        tokens,
        norm_gain[None],
        w_qkv.transpose(1, 0, 2),
        leaf_kv[:, :, 0].reshape(-1, WIDTH),
        leaf_kv[:, :, 1].reshape(-1, WIDTH),
    )
    q_peer = lax.ppermute(q, "c", [(0, 1), (1, 0)])
    along_z, outgoing, q_peer = lax.optimization_barrier((along_z, outgoing, q_peer))
    near = lax.ppermute(along_z, "x", [(i, i ^ 1) for i in range(4)])
    pair = jnp.concatenate([along_z, near], axis=0)
    far = lax.ppermute(pair, "x", [(i, i ^ 2) for i in range(4)])
    incoming = lax.all_to_all(outgoing, REQ, 0, 0, tiled=True)
    me = lax.axis_index(REQ)
    owned = jnp.sum(jnp.where(node_owner == me, branch_len, 0)).reshape(1)
    answer = pl.pallas_call(
        branch_kernel,
        out_shape=sds(nodes * PACKET, BF16),
        in_specs=[SM, VM, VM, VM],
        out_specs=VM,
        compiler_params=PARAMS,
        name="branch",
        cost_estimate=pl.CostEstimate(flops=5000000000, transcendentals=0, bytes_accessed=0),
    )(owned, incoming, branch_kv[0, :, 0], branch_kv[0, :, 1])
    _, far = lax.optimization_barrier((answer, far))
    back = lax.all_to_all(answer.reshape(nodes, PACKET // 2, 2, WIDTH), REQ, 0, 0, tiled=True)

    keys = (pair.shape[0] + far.shape[0]) // 2
    m_rest, t_rest, o_rest, send = pl.pallas_call(
        root_kernel,
        out_shape=[sds(rows, F32)] * 3 + [sds(2 * rows, F32)],
        in_specs=[VM] * 7,
        out_specs=[VM] * 4,
        scratch_shapes=[pltpu.VMEM((4 * rows, keys), F32)],
        compiler_params=PARAMS,
        name="root",
    )(q, q_peer, m_local, t_local, o_local, pair, far)
    peer = lax.ppermute(send, "c", [(0, 1), (1, 0)])

    terms = pl.pallas_call(
        finish_kernel,
        out_shape=sds(tensor * rows, BF16),
        in_specs=[VM] * 8,
        out_specs=VM,
        compiler_params=PARAMS,
        name="finish",
    )(back.reshape(nodes * PACKET, WIDTH), peer, pos, use, m_rest, t_rest, o_rest, w_out)
    shares = lax.all_to_all(terms, "y", 0, 0, tiled=True)
    return pl.pallas_call(
        add_kernel,
        out_shape=sds(rows, BF16),
        in_specs=[VM],
        out_specs=VM,
        compiler_params=PARAMS,
        name="add",
    )(shares)


def solution(mesh):
    split = Mesh(mesh.devices.reshape(8, 4, 2, 8), REQ + ("y",))
    placed = (
        P(REQ, None),
        P(),
        P(None, None, "y"),
        P("y", None),
        P(REQ, None, "y"),
        P(REQ, None, None, "y"),
        P(REQ, None, None, "y"),
        P(REQ, None),
        P(),
        P(),
        P(REQ),
        P(REQ),
    )
    return jax.shard_map(
        local, mesh=split, in_specs=placed, out_specs=P(REQ, "y"), check_vma=False
    )
```

```python
import jax
import jax.numpy as jnp
from jax import lax
from jax.experimental import pallas as pl
from jax.experimental.pallas import tpu as pltpu
from jax.sharding import Mesh
from jax.sharding import PartitionSpec as P

HD = 64
WIDTH = 128
DRAFTS = 4
CAPACITY = 2
PACK = 72
NEG = -1e30
F32 = jnp.float32
BF16 = jnp.bfloat16
REQ = ("z", "x", "c")
VM = pl.BlockSpec(memory_space=pltpu.VMEM)
SM = pl.BlockSpec(memory_space=pltpu.SMEM)
HB = pl.BlockSpec(memory_space=pltpu.HBM)
PARAMS = pltpu.CompilerParams(vmem_limit_bytes=48 * 1024 * 1024)


def iota(shape, dim):
    return lax.broadcasted_iota(jnp.int32, shape, dim)


def low_lanes(shape):
    return iota(shape, len(shape) - 1) < HD


def stack_heads(q):
    low = low_lanes(q.shape)
    zero = jnp.zeros_like(q)
    return jnp.concatenate([jnp.where(low, q, zero), jnp.where(low, zero, q)], axis=0)


def merge_heads(x):
    n = x.shape[0] // 2
    return jnp.where(low_lanes((n, WIDTH)), x[:n], x[n:])


def dot_nt(a, b):
    return lax.dot_general(a, b, (((1,), (1,)), ((), ())), preferred_element_type=F32)


def sds(rows, dtype):
    return jax.ShapeDtypeStruct((rows, WIDTH), dtype)


def places_of(branch_s, owner_s, count_s, requests):
    targets = [owner_s[branch_s[r]] for r in range(requests)]
    for r in range(requests):
        count_s[targets[r]] = 0
    places = []
    for r in range(requests):
        earlier = count_s[targets[r]]
        count_s[targets[r]] = earlier + 1
        places.append(targets[r] * CAPACITY + earlier)
    return places


def local_group(q, own_k, own_v, leaf_k, leaf_v, leaf_row, new_row):
    rows = q.shape[0]
    stacked = stack_heads(q)
    leaf_two = jnp.concatenate([leaf_row, leaf_row], axis=0)
    new_two = jnp.concatenate([new_row, new_row], axis=0)
    both = 2 * rows
    span = leaf_k.shape[0]
    score_leaf = dot_nt(stacked, leaf_k)
    score_own = dot_nt(stacked, own_k)
    key = iota((both, span), 1)
    request_of = (iota((both, span), 0) & (rows - 1)) >> 2
    leaf_wide = jnp.concatenate([leaf_two] * (span // WIDTH), axis=1)
    ok_leaf = ((key >> 4) == request_of) & ((key & 15) < leaf_wide)
    key = iota((both, rows), 1)
    query = iota((both, rows), 0) & (rows - 1)
    ok_own = (
        ((key >> 2) == (query >> 2))
        & ((key & 3) <= (query & 3))
        & ((key & 3) < new_two[:, :rows])
    )
    score_leaf = jnp.where(ok_leaf, score_leaf, NEG)
    score_own = jnp.where(ok_own, score_own, NEG)
    peak = jnp.maximum(
        jnp.max(score_leaf, axis=1, keepdims=True), jnp.max(score_own, axis=1, keepdims=True)
    )
    w_leaf = jnp.where(ok_leaf, jnp.exp(score_leaf - peak), 0.0)
    w_own = jnp.where(ok_own, jnp.exp(score_own - peak), 0.0)
    total = jnp.sum(w_leaf, axis=1, keepdims=True) + jnp.sum(w_own, axis=1, keepdims=True)
    weighted = jnp.dot(w_leaf.astype(BF16), leaf_v, preferred_element_type=F32) + jnp.dot(
        w_own.astype(BF16), own_v, preferred_element_type=F32
    )
    return (
        merge_heads(jnp.broadcast_to(peak, (both, WIDTH))),
        merge_heads(jnp.broadcast_to(total, (both, WIDTH))),
        merge_heads(weighted),
    )


def normed_rows(tok_ref, gain_ref):
    x = tok_ref[...].astype(F32)
    scale = lax.rsqrt(jnp.mean(x * x, axis=1, keepdims=True) + 1e-05)
    return (x * scale * gain_ref[...]).astype(BF16)


def front_kernel(
    branch_hbm, owner_hbm, tok_hbm, gain_hbm, w_hbm, q_ref, out_ref, branch_s, owner_s, tok_ref, gain_ref, w_ref, count_s, sem
):
    rows = tok_ref.shape[0]
    requests = rows // DRAFTS
    pairs = (
        (branch_hbm, branch_s),
        (owner_hbm, owner_s),
        (tok_hbm, tok_ref),
        (gain_hbm, gain_ref),
        (w_hbm.at[0], w_ref),
    )
    fetches = [pltpu.make_async_copy(a, b, sem.at[n]) for n, (a, b) in enumerate(pairs)]
    for fetch in fetches:
        fetch.start()
    fetches[0].wait()
    fetches[1].wait()
    places = places_of(branch_s, owner_s, count_s, requests)
    lane = iota((8, WIDTH), 1) >> 2
    slots = jnp.zeros((8, WIDTH), jnp.int32)
    for r in range(requests):
        slots = jnp.where(lane == r, places[r], slots)
    fetches[2].wait()
    fetches[3].wait()
    normed = normed_rows(tok_ref, gain_ref)
    fetches[4].wait()
    q = jnp.dot(normed, w_ref[...], preferred_element_type=F32).astype(BF16)
    q = q * jnp.asarray(HD**-0.5, BF16)
    q_ref[...] = q
    block = jnp.concatenate([q.astype(F32), slots.astype(F32)], axis=0)
    out_ref[...] = jnp.concatenate([block] * (out_ref.shape[0] // PACK), axis=0).astype(BF16)


def routes(got, me):
    found = []
    for s in range(got.shape[0]):
        place = jnp.broadcast_to(got[s, 64:72][:1, :64], (64, 64)).astype(jnp.int32)
        at = ((place >> 1) & 7) * 8 + (place & 1) * DRAFTS + (iota((64, 64), 1) & 3)
        here = ((place >> 4) == me) & (iota((64, 64), 0) == at)
        found.append(jnp.where(here, 1.0, 0.0))
    return found


def select_kernel(me_s, got_ref, out_ref):
    planes = out_ref.shape[0] // 64
    got = got_ref[...].astype(F32).reshape(-1, PACK, WIDTH)
    chosen = [
        jnp.dot(
            route.astype(BF16), got[s, :64].astype(BF16), preferred_element_type=F32
        ).reshape(planes, 8, WIDTH)
        for s, route in enumerate(routes(got, me_s[0]))
    ]
    out_ref[...] = jnp.concatenate(chosen, axis=1).reshape(-1, WIDTH).astype(BF16)


def attend(blocks, keys, values_t, valid):
    count = blocks[0].shape[0]
    first = iota((WIDTH, count), 0) < HD
    scores = [dot_nt(keys, stack_heads(q)) for q in blocks]
    if valid is not None:
        scores = [jnp.where(valid, score, NEG) for score in scores]
    peaks = [jnp.max(score, axis=0, keepdims=True) for score in scores]
    weights, totals = [], []
    for score, peak in zip(scores, peaks):
        weight = jnp.exp(score - peak)
        totals.append(jnp.sum(weight, axis=0, keepdims=True))
        weights.append(weight.astype(BF16))
    for weight, peak, total in zip(weights, peaks, totals):
        mean = jnp.dot(values_t, weight, preferred_element_type=F32) / total
        mean = jnp.where(first, mean[:, :count], mean[:, count:]).T
        yield mean, peak + jnp.log(total)


def three_terms(level, term):
    one = level.astype(BF16).astype(F32)
    two = (level - one).astype(BF16).astype(F32)
    three = level - one - two
    return jnp.where(term == 0, one, jnp.where(term == 1, two, jnp.where(term == 2, three, 0.0)))


def own_lanes(shape):
    return (iota(shape, 1) >> 4) == (iota(shape, 0) & 7)


def level_sum(second):
    row, column = iota((WIDTH, WIDTH), 0), iota((WIDTH, WIDTH), 1)
    head = ((row >> 3) & 1) == (column >> 6)
    term = (row & 7) == 3 if second else (row & 7) < 3
    return jnp.where(head & term, 1.0, 0.0).astype(BF16)


def branch_kernel(len_s, q_ref, k_ref, vt_ref, out_hbm, out_ref, sem):
    span = k_ref.shape[0]
    block = 256
    size = block // 64 * PACK
    valid = iota((span, 2 * block), 0) < len_s[0]
    to = iota((size, 2 * block), 0)
    frm = iota((size, 2 * block), 1)
    query = frm & (block - 1)
    goal = (query >> 6) * PACK + jnp.where(frm < block, query & 63, 64 + ((query >> 3) & 7))
    spread = jnp.where(to == goal, 1.0, 0.0).astype(BF16)
    repeat = jnp.where((iota((16, WIDTH), 1) & 15) == iota((16, WIDTH), 0), 1.0, 0.0).astype(BF16)
    mine = own_lanes((block, WIDTH))
    term = iota((8, 2 * block), 0)
    blocks = [q_ref[b * block : (b + 1) * block] for b in range(q_ref.shape[0] // block)]
    sends = []
    for b, (mean, level) in enumerate(attend(blocks, k_ref[...], vt_ref[...], valid)):
        terms = jnp.where(term == 3, 1.0, three_terms(level, term))
        terms = jnp.concatenate([terms[:, :block], terms[:, block:]], axis=0).astype(BF16)
        levels = lax.dot_general(
            terms, repeat, (((0,), (0,)), ((), ())), preferred_element_type=F32
        )
        levels = jnp.where(mine, levels, 0.0)
        packed = jnp.dot(
            spread, jnp.concatenate([mean, levels], axis=0).astype(BF16), preferred_element_type=F32
        )
        out_ref[b] = packed.astype(BF16)
        sends.append(
            pltpu.make_async_copy(out_ref.at[b], out_hbm.at[pl.ds(b * size, size)], sem.at[b])
        )
        sends[b].start()
    for send in sends:
        send.wait()


def root_kernel(got_ref, rows_ref, more_ref, mean_ref, level_ref):
    sort = (iota((128, 128), 0) & 63) * 2 + (iota((128, 128), 0) >> 6) == iota((128, 128), 1)
    sort = jnp.where(sort, 1.0, 0.0).astype(BF16)
    wide = jnp.concatenate(
        [ref[s : s + 128] for ref in (rows_ref, more_ref) for s in range(0, ref.shape[0], 128)],
        axis=1,
    )
    kinds = jnp.dot(sort, wide, preferred_element_type=F32)
    keys, values = (
        jnp.concatenate(
            [kinds[r : r + 64, s : s + WIDTH] for s in range(0, wide.shape[1], WIDTH)], axis=0
        )
        for r in (0, 64)
    )
    got = got_ref[...].astype(F32).reshape(-1, PACK, WIDTH)
    block = 256
    q = got[:, :64].reshape(-1, WIDTH).astype(BF16)
    blocks = [q[s : s + block] for s in range(0, q.shape[0], block)]
    first = iota((WIDTH, block), 0) < HD
    found = attend(blocks, keys.astype(BF16), values.T.astype(BF16), None)
    for b, (mean, level) in enumerate(found):
        mean_ref[b * block : (b + 1) * block] = mean
        level_ref[b * block : (b + 1) * block] = jnp.where(
            first, level[:, :block], level[:, block:]
        ).T


def merge_kernel(me_s, got_ref, back_ref, mean_ref, level_ref, out_ref):
    got = got_ref[...].astype(F32).reshape(-1, PACK, WIDTH)
    back = back_ref[...].astype(F32).reshape(-1, PACK, WIDTH)
    planes = back.shape[0]
    mine = own_lanes((64, WIDTH))
    picked = []
    for s, route in enumerate(routes(got, me_s[0])):
        part = back[:, s * 8 : s * 8 + 8].reshape(64, WIDTH)
        shared = jnp.broadcast_to(back[:, 64 + s : 65 + s], (planes, 8, WIDTH)).reshape(64, WIDTH)
        both = jnp.concatenate([part, jnp.where(mine, shared, 0.0)], axis=1).astype(BF16)
        picked.append(jnp.dot(route.T.astype(BF16), both, preferred_element_type=F32))
    picked = jnp.concatenate(picked, axis=0)
    part = picked[:, :WIDTH]
    sums = jnp.dot(
        picked[:, WIDTH:].astype(BF16),
        jnp.concatenate([level_sum(False), level_sum(True)], axis=1),
        preferred_element_type=F32,
    )
    level = jnp.where(sums[:, WIDTH:] > 0.5, sums[:, :WIDTH], NEG)
    high = jnp.maximum(level, level_ref[...])
    scale_root = jnp.exp(level_ref[...] - high)
    scale_branch = jnp.exp(level - high)
    total = scale_root + scale_branch
    mean = (mean_ref[...] * scale_root + part * scale_branch) / total
    level = high + jnp.log(total)
    lane = iota(level.shape, 1)
    level = jnp.where(((lane >> 3) & 1) == 0, level[:, :1], level[:, HD : HD + 1])
    levels = jnp.where(own_lanes(level.shape), three_terms(level, lane & 7), 0.0)
    levels = jnp.sum(levels.reshape(-1, 8, WIDTH), axis=1).reshape(-1, 8, WIDTH)
    packed = jnp.concatenate([mean.reshape(-1, 64, WIDTH), levels], axis=1)
    out_ref[...] = packed.reshape(-1, WIDTH).astype(BF16)


def local_kernel(
    leaf_len_s, new_s, tok_ref, gain_ref, w_ref, q_ref, leaf_k_ref, leaf_v_ref, m_ref, t_ref, o_ref, new_ref
):
    rows = tok_ref.shape[0]
    row = iota((rows, WIDTH), 0)
    leaf_row = jnp.zeros((rows, WIDTH), jnp.int32)
    new_row = jnp.zeros((rows, WIDTH), jnp.int32)
    for r in range(rows // DRAFTS):
        mine = (row >> 2) == r
        leaf_row = jnp.where(mine, leaf_len_s[r], leaf_row)
        new_row = jnp.where(mine, new_s[r], new_row)
    new_ref[...] = new_row
    normed = normed_rows(tok_ref, gain_ref)

    def project(n):
        return jnp.dot(normed, w_ref[n], preferred_element_type=F32).astype(BF16)

    m_ref[...], t_ref[...], o_ref[...] = local_group(
        q_ref[...], project(1), project(2), leaf_k_ref[...], leaf_v_ref[...], leaf_row, new_row
    )


def finish_kernel(parts_ref, new_ref, m_ref, t_ref, o_ref, w_ref, out_ref):
    rows = new_ref.shape[0]
    parts = parts_ref[...].astype(F32).reshape(-1, PACK, WIDTH)
    count = parts.shape[0]
    shared = jnp.broadcast_to(parts[:, 64:, None], (count, 8, 8, WIDTH)).reshape(-1, WIDTH)
    shared = jnp.where(own_lanes(shared.shape), shared, 0.0).astype(BF16)
    levels = jnp.dot(shared, level_sum(False), preferred_element_type=F32).reshape(count, rows, WIDTH)
    high = jnp.maximum(jnp.max(levels, axis=0), m_ref[...])
    scale = jnp.exp(m_ref[...] - high)
    total = t_ref[...] * scale
    weighted = o_ref[...] * scale
    for s in range(count):
        scale = jnp.exp(levels[s] - high)
        total = total + scale
        weighted = weighted + parts[s, :64] * scale
    used = (iota((rows, WIDTH), 0) & 3) < new_ref[...]
    attention = jnp.where(used, weighted / total, 0.0).astype(BF16)
    terms = jnp.dot(attention, w_ref[...], preferred_element_type=F32).astype(BF16)
    for s in range(w_ref.shape[1] // WIDTH):
        out_ref[s * rows : (s + 1) * rows] = terms[:, s * WIDTH : (s + 1) * WIDTH]


def local(
    tokens,
    norm_gain,
    w_qkv,
    w_out,
    root_kv,
    branch_kv,
    leaf_kv,
    branch,
    node_owner,
    branch_len,
    leaf_len,
    new_count,
):
    rows = tokens.shape[0]
    nodes = node_owner.shape[0]
    tensor = w_out.shape[1] // WIDTH
    column = lax.axis_size("z")
    plane = nodes // column

    def call(kernel, name, out_shape, specs, outs, scratch=(), **extra):
        return pl.pallas_call(
            kernel,
            out_shape=out_shape,
            in_specs=specs,
            out_specs=outs,
            scratch_shapes=scratch,
            compiler_params=PARAMS,
            name=name,
            **extra,
        )

    def after(first, value):
        return lax.optimization_barrier((first, value))[1]

    def swap(value, axis, distance):
        size = lax.axis_size(axis)
        return lax.ppermute(value, axis, [(i, i ^ distance) for i in range(size)])

    gain = norm_gain[None]
    weights = w_qkv.transpose(1, 0, 2)
    me = lax.axis_index("z").reshape(1)
    q, sent = call(
        front_kernel,
        "front",
        [sds(rows, BF16), sds(column * PACK, BF16)],
        [HB] * 5,
        [VM] * 2,
        [
            pltpu.SMEM((rows // DRAFTS,), jnp.int32),
            pltpu.SMEM((nodes,), jnp.int32),
            pltpu.VMEM(tokens.shape, BF16),
            pltpu.VMEM(gain.shape, F32),
            pltpu.VMEM(weights.shape[1:], BF16),
            pltpu.SMEM((nodes,), jnp.int32),
            pltpu.SemaphoreType.DMA((5,)),
        ],
    )(*[pltpu.with_memory_space_constraint(a, pltpu.HBM) for a in (branch[:, 0], node_owner, tokens, gain, weights)])
    got = lax.all_to_all(sent, "z", 0, 0, tiled=True)
    root_rows = after(sent, root_kv.reshape(-1, WIDTH))
    pair = jnp.concatenate([root_rows, swap(root_rows, "c", 1)], axis=0)
    middle = swap(pair, "x", 1)
    asked = call(
        select_kernel, "select", sds(plane * 64, BF16), [SM, VM], VM
    )(me, got)
    incoming = lax.all_to_all(asked, ("x", "c"), 0, 0, tiled=True)
    quad = jnp.concatenate([pair, after(asked, middle)], axis=0)
    near = swap(quad, "x", 2)
    owner = lax.axis_index(REQ)
    owned = jnp.sum(jnp.where(node_owner == owner, branch_len, 0)).reshape(1)
    answer = call(
        branch_kernel,
        "branch",
        sds(plane * PACK, BF16),
        [SM, VM, VM, VM],
        HB,
        [pltpu.VMEM((2, plane * PACK // 2, WIDTH), BF16), pltpu.SemaphoreType.DMA((2,))],
        cost_estimate=pl.CostEstimate(flops=5000000000, transcendentals=0, bytes_accessed=0),
    )(owned, incoming, branch_kv[0, :, 0], branch_kv[0, :, 1].T)
    back = lax.all_to_all(answer, ("x", "c"), 0, 0, tiled=True)
    root_mean, root_level = call(
        root_kernel,
        "root",
        [sds(column * 64, F32)] * 2,
        [VM] * 3,
        [VM] * 2,
    )(got, quad, after(answer, near))
    merged = call(
        merge_kernel,
        "merge",
        sds(column * PACK, BF16),
        [SM] + [VM] * 4,
        VM,
    )(me, got, back, root_mean, root_level)
    parts = lax.all_to_all(merged, "z", 0, 0, tiled=True)
    m_local, t_local, o_local, new_row = call(
        local_kernel,
        "local",
        [sds(rows, F32)] * 3 + [sds(rows, jnp.int32)],
        [SM] * 2 + [VM] * 6,
        [VM] * 4,
    )(
        leaf_len,
        new_count,
        tokens,
        gain,
        weights,
        after(merged, q),
        leaf_kv[:, :, 0].reshape(-1, WIDTH),
        leaf_kv[:, :, 1].reshape(-1, WIDTH),
    )
    terms = call(
        finish_kernel, "finish", sds(tensor * rows, BF16), [VM] * 6, VM
    )(parts, new_row, m_local, t_local, o_local, w_out)
    shares = lax.all_to_all(terms, "y", 0, 0, tiled=True)
    return jnp.sum(shares.reshape(tensor, rows, WIDTH).astype(F32), axis=0).astype(BF16)


def solution(mesh):
    split = Mesh(mesh.devices.reshape(8, 4, 2, 8), REQ + ("y",))
    placed = (
        P(REQ, None),
        P(),
        P(None, None, "y"),
        P("y", None),
        P(REQ, None, "y"),
        P(REQ, None, None, "y"),
        P(REQ, None, None, "y"),
        P(REQ, None),
        P(),
        P(),
        P(REQ),
        P(REQ),
    )
    return jax.shard_map(
        local, mesh=split, in_specs=placed, out_specs=P(REQ, "y"), check_vma=False
    )
```

```python
import jax
import jax.numpy as jnp
from jax import lax
from jax.experimental import pallas as pl
from jax.experimental.pallas import tpu as pltpu
from jax.sharding import Mesh
from jax.sharding import PartitionSpec as P

HD = 64
WIDTH = 128
DRAFTS = 4
CAPACITY = 2
PACK = 72
NEG = -1e30
F32 = jnp.float32
BF16 = jnp.bfloat16
REQ = ("z", "x", "c")
VM = pl.BlockSpec(memory_space=pltpu.VMEM)
SM = pl.BlockSpec(memory_space=pltpu.SMEM)
HB = pl.BlockSpec(memory_space=pltpu.HBM)
PARAMS = pltpu.CompilerParams(vmem_limit_bytes=48 * 1024 * 1024)


def iota(shape, dim):
    return lax.broadcasted_iota(jnp.int32, shape, dim)


def low_lanes(shape):
    return iota(shape, len(shape) - 1) < HD


def stack_heads(q):
    low = low_lanes(q.shape)
    zero = jnp.zeros_like(q)
    return jnp.concatenate([jnp.where(low, q, zero), jnp.where(low, zero, q)], axis=0)


def merge_heads(x):
    n = x.shape[0] // 2
    return jnp.where(low_lanes((n, WIDTH)), x[:n], x[n:])


def dot_nt(a, b):
    return lax.dot_general(a, b, (((1,), (1,)), ((), ())), preferred_element_type=F32)


def sds(rows, dtype):
    return jax.ShapeDtypeStruct((rows, WIDTH), dtype)


def places_of(branch_s, owner_s, count_s, requests):
    targets = [owner_s[branch_s[r]] for r in range(requests)]
    for r in range(requests):
        count_s[targets[r]] = 0
    places = []
    for r in range(requests):
        earlier = count_s[targets[r]]
        count_s[targets[r]] = earlier + 1
        places.append(targets[r] * CAPACITY + earlier)
    return places


def local_group(q, own_k, own_v, leaf_k, leaf_v, leaf_row, new_row):
    rows = q.shape[0]
    stacked = stack_heads(q)
    leaf_two = jnp.concatenate([leaf_row, leaf_row], axis=0)
    new_two = jnp.concatenate([new_row, new_row], axis=0)
    both = 2 * rows
    span = leaf_k.shape[0]
    score_leaf = dot_nt(stacked, leaf_k)
    score_own = dot_nt(stacked, own_k)
    key = iota((both, span), 1)
    request_of = (iota((both, span), 0) & (rows - 1)) >> 2
    leaf_wide = jnp.concatenate([leaf_two] * (span // WIDTH), axis=1)
    ok_leaf = ((key >> 4) == request_of) & ((key & 15) < leaf_wide)
    key = iota((both, rows), 1)
    query = iota((both, rows), 0) & (rows - 1)
    ok_own = (
        ((key >> 2) == (query >> 2))
        & ((key & 3) <= (query & 3))
        & ((key & 3) < new_two[:, :rows])
    )
    score_leaf = jnp.where(ok_leaf, score_leaf, NEG)
    score_own = jnp.where(ok_own, score_own, NEG)
    peak = jnp.maximum(
        jnp.max(score_leaf, axis=1, keepdims=True), jnp.max(score_own, axis=1, keepdims=True)
    )
    w_leaf = jnp.where(ok_leaf, jnp.exp(score_leaf - peak), 0.0)
    w_own = jnp.where(ok_own, jnp.exp(score_own - peak), 0.0)
    total = jnp.sum(w_leaf, axis=1, keepdims=True) + jnp.sum(w_own, axis=1, keepdims=True)
    weighted = jnp.dot(w_leaf.astype(BF16), leaf_v, preferred_element_type=F32) + jnp.dot(
        w_own.astype(BF16), own_v, preferred_element_type=F32
    )
    return (
        merge_heads(jnp.broadcast_to(peak, (both, WIDTH))),
        merge_heads(jnp.broadcast_to(total, (both, WIDTH))),
        merge_heads(weighted),
    )


def normed_rows(tok_ref, gain_ref):
    x = tok_ref[...].astype(F32)
    scale = lax.rsqrt(jnp.mean(x * x, axis=1, keepdims=True) + 1e-05)
    return (x * scale * gain_ref[...]).astype(BF16)


def front_kernel(
    branch_hbm, owner_hbm, tok_hbm, gain_hbm, w_hbm, q_ref, out_ref, branch_s, owner_s, tok_ref, gain_ref, w_ref, count_s, sem
):
    rows = tok_ref.shape[0]
    requests = rows // DRAFTS
    pairs = (
        (branch_hbm, branch_s),
        (owner_hbm, owner_s),
        (tok_hbm, tok_ref),
        (gain_hbm, gain_ref),
        (w_hbm.at[0], w_ref),
    )
    fetches = [pltpu.make_async_copy(a, b, sem.at[n]) for n, (a, b) in enumerate(pairs)]
    for fetch in fetches:
        fetch.start()
    fetches[0].wait()
    fetches[1].wait()
    places = places_of(branch_s, owner_s, count_s, requests)
    lane = iota((8, WIDTH), 1) >> 2
    slots = jnp.zeros((8, WIDTH), jnp.int32)
    for r in range(requests):
        slots = jnp.where(lane == r, places[r], slots)
    fetches[2].wait()
    fetches[3].wait()
    normed = normed_rows(tok_ref, gain_ref)
    fetches[4].wait()
    q = jnp.dot(normed, w_ref[...], preferred_element_type=F32).astype(BF16)
    q = q * jnp.asarray(HD**-0.5, BF16)
    q_ref[...] = q
    block = jnp.concatenate([q.astype(F32), slots.astype(F32)], axis=0)
    out_ref[...] = jnp.concatenate([block] * (out_ref.shape[0] // PACK), axis=0).astype(BF16)


def routes(got, me):
    found = []
    for s in range(got.shape[0]):
        place = jnp.broadcast_to(got[s, 64:72][:1, :64], (64, 64)).astype(jnp.int32)
        at = ((place >> 1) & 7) * 8 + (place & 1) * DRAFTS + (iota((64, 64), 1) & 3)
        here = ((place >> 4) == me) & (iota((64, 64), 0) == at)
        found.append(jnp.where(here, 1.0, 0.0))
    return found


def select_kernel(me_s, got_ref, out_ref):
    planes = out_ref.shape[0] // 64
    got = got_ref[...].astype(F32).reshape(-1, PACK, WIDTH)
    chosen = [
        jnp.dot(
            route.astype(BF16), got[s, :64].astype(BF16), preferred_element_type=F32
        ).reshape(planes, 8, WIDTH)
        for s, route in enumerate(routes(got, me_s[0]))
    ]
    out_ref[...] = jnp.concatenate(chosen, axis=1).reshape(-1, WIDTH).astype(BF16)


def attend(blocks, keys, values_t, valid):
    count = blocks[0].shape[0]
    first = iota((WIDTH, count), 0) < HD
    scores = [dot_nt(keys, stack_heads(q)) for q in blocks]
    if valid is not None:
        scores = [jnp.where(valid, score, NEG) for score in scores]
    peaks = [jnp.max(score, axis=0, keepdims=True) for score in scores]
    weights, totals = [], []
    for score, peak in zip(scores, peaks):
        weight = jnp.exp(score - peak)
        totals.append(jnp.sum(weight, axis=0, keepdims=True))
        weights.append(weight.astype(BF16))
    for weight, peak, total in zip(weights, peaks, totals):
        mean = jnp.dot(values_t, weight, preferred_element_type=F32) / total
        mean = jnp.where(first, mean[:, :count], mean[:, count:]).T
        yield mean, peak + jnp.log(total)


def three_terms(level, term):
    one = level.astype(BF16).astype(F32)
    two = (level - one).astype(BF16).astype(F32)
    three = level - one - two
    return jnp.where(term == 0, one, jnp.where(term == 1, two, jnp.where(term == 2, three, 0.0)))


def own_lanes(shape):
    return (iota(shape, 1) >> 4) == (iota(shape, 0) & 7)


def level_sum(second):
    row, column = iota((WIDTH, WIDTH), 0), iota((WIDTH, WIDTH), 1)
    head = ((row >> 3) & 1) == (column >> 6)
    term = (row & 7) == 3 if second else (row & 7) < 3
    return jnp.where(head & term, 1.0, 0.0).astype(BF16)


def branch_kernel(me_s, owner_ref, len_ref, q_ref, k_ref, vt_ref, out_hbm, out_ref, sem):
    span = k_ref.shape[0]
    block = 256
    size = block // 64 * PACK
    length = jnp.where(owner_ref[...] == me_s[0], len_ref[...], 0)
    length = jnp.sum(length, axis=1, keepdims=True)
    valid = iota((span, 2 * block), 0) < length
    to = iota((size, 2 * block), 0)
    frm = iota((size, 2 * block), 1)
    query = frm & (block - 1)
    goal = (query >> 6) * PACK + jnp.where(frm < block, query & 63, 64 + ((query >> 3) & 7))
    spread = jnp.where(to == goal, 1.0, 0.0).astype(BF16)
    repeat = jnp.where((iota((16, WIDTH), 1) & 15) == iota((16, WIDTH), 0), 1.0, 0.0).astype(BF16)
    mine = own_lanes((block, WIDTH))
    term = iota((8, 2 * block), 0)
    blocks = [q_ref[b * block : (b + 1) * block] for b in range(q_ref.shape[0] // block)]
    sends = []
    for b, (mean, level) in enumerate(attend(blocks, k_ref[...], vt_ref[...], valid)):
        terms = jnp.where(term == 3, 1.0, three_terms(level, term))
        terms = jnp.concatenate([terms[:, :block], terms[:, block:]], axis=0).astype(BF16)
        levels = lax.dot_general(
            terms, repeat, (((0,), (0,)), ((), ())), preferred_element_type=F32
        )
        levels = jnp.where(mine, levels, 0.0)
        packed = jnp.dot(
            spread, jnp.concatenate([mean, levels], axis=0).astype(BF16), preferred_element_type=F32
        )
        out_ref[b] = packed.astype(BF16)
        sends.append(
            pltpu.make_async_copy(out_ref.at[b], out_hbm.at[pl.ds(b * size, size)], sem.at[b])
        )
        sends[b].start()
    for send in sends:
        send.wait()


def root_kernel(got_ref, rows_ref, more_ref, mean_ref, level_ref):
    sort = (iota((128, 128), 0) & 63) * 2 + (iota((128, 128), 0) >> 6) == iota((128, 128), 1)
    sort = jnp.where(sort, 1.0, 0.0).astype(BF16)
    wide = jnp.concatenate(
        [ref[s : s + 128] for ref in (rows_ref, more_ref) for s in range(0, ref.shape[0], 128)],
        axis=1,
    )
    kinds = jnp.dot(sort, wide, preferred_element_type=F32)
    keys, values = (
        jnp.concatenate(
            [kinds[r : r + 64, s : s + WIDTH] for s in range(0, wide.shape[1], WIDTH)], axis=0
        )
        for r in (0, 64)
    )
    got = got_ref[...].astype(F32).reshape(-1, PACK, WIDTH)
    block = 256
    q = got[:, :64].reshape(-1, WIDTH).astype(BF16)
    blocks = [q[s : s + block] for s in range(0, q.shape[0], block)]
    first = iota((WIDTH, block), 0) < HD
    found = attend(blocks, keys.astype(BF16), values.T.astype(BF16), None)
    for b, (mean, level) in enumerate(found):
        mean_ref[b * block : (b + 1) * block] = mean
        level_ref[b * block : (b + 1) * block] = jnp.where(
            first, level[:, :block], level[:, block:]
        ).T


def merge_kernel(me_s, got_ref, back_ref, mean_ref, level_ref, out_ref):
    got = got_ref[...].astype(F32).reshape(-1, PACK, WIDTH)
    back = back_ref[...].astype(F32).reshape(-1, PACK, WIDTH)
    planes = back.shape[0]
    mine = own_lanes((64, WIDTH))
    picked = []
    for s, route in enumerate(routes(got, me_s[0])):
        part = back[:, s * 8 : s * 8 + 8].reshape(64, WIDTH)
        shared = jnp.broadcast_to(back[:, 64 + s : 65 + s], (planes, 8, WIDTH)).reshape(64, WIDTH)
        both = jnp.concatenate([part, jnp.where(mine, shared, 0.0)], axis=1).astype(BF16)
        picked.append(jnp.dot(route.T.astype(BF16), both, preferred_element_type=F32))
    picked = jnp.concatenate(picked, axis=0)
    part = picked[:, :WIDTH]
    sums = jnp.dot(
        picked[:, WIDTH:].astype(BF16),
        jnp.concatenate([level_sum(False), level_sum(True)], axis=1),
        preferred_element_type=F32,
    )
    level = jnp.where(sums[:, WIDTH:] > 0.5, sums[:, :WIDTH], NEG)
    high = jnp.maximum(level, level_ref[...])
    scale_root = jnp.exp(level_ref[...] - high)
    scale_branch = jnp.exp(level - high)
    total = scale_root + scale_branch
    mean = (mean_ref[...] * scale_root + part * scale_branch) / total
    level = high + jnp.log(total)
    lane = iota(level.shape, 1)
    level = jnp.where(((lane >> 3) & 1) == 0, level[:, :1], level[:, HD : HD + 1])
    levels = jnp.where(own_lanes(level.shape), three_terms(level, lane & 7), 0.0)
    levels = jnp.sum(levels.reshape(-1, 8, WIDTH), axis=1).reshape(-1, 8, WIDTH)
    packed = jnp.concatenate([mean.reshape(-1, 64, WIDTH), levels], axis=1)
    out_ref[...] = packed.reshape(-1, WIDTH).astype(BF16)


def local_kernel(
    leaf_len_s, new_s, tok_ref, gain_ref, w_ref, q_ref, leaf_k_ref, leaf_v_ref, m_ref, t_ref, o_ref, new_ref
):
    rows = tok_ref.shape[0]
    row = iota((rows, WIDTH), 0)
    leaf_row = jnp.zeros((rows, WIDTH), jnp.int32)
    new_row = jnp.zeros((rows, WIDTH), jnp.int32)
    for r in range(rows // DRAFTS):
        mine = (row >> 2) == r
        leaf_row = jnp.where(mine, leaf_len_s[r], leaf_row)
        new_row = jnp.where(mine, new_s[r], new_row)
    new_ref[...] = new_row
    normed = normed_rows(tok_ref, gain_ref)

    def project(n):
        return jnp.dot(normed, w_ref[n], preferred_element_type=F32).astype(BF16)

    m_ref[...], t_ref[...], o_ref[...] = local_group(
        q_ref[...], project(1), project(2), leaf_k_ref[...], leaf_v_ref[...], leaf_row, new_row
    )


def finish_kernel(parts_ref, new_ref, m_ref, t_ref, o_ref, w_ref, out_ref):
    rows = new_ref.shape[0]
    parts = parts_ref[...].astype(F32).reshape(-1, PACK, WIDTH)
    count = parts.shape[0]
    shared = jnp.broadcast_to(parts[:, 64:, None], (count, 8, 8, WIDTH)).reshape(-1, WIDTH)
    shared = jnp.where(own_lanes(shared.shape), shared, 0.0).astype(BF16)
    levels = jnp.dot(shared, level_sum(False), preferred_element_type=F32).reshape(count, rows, WIDTH)
    high = jnp.maximum(jnp.max(levels, axis=0), m_ref[...])
    scale = jnp.exp(m_ref[...] - high)
    total = t_ref[...] * scale
    weighted = o_ref[...] * scale
    for s in range(count):
        scale = jnp.exp(levels[s] - high)
        total = total + scale
        weighted = weighted + parts[s, :64] * scale
    used = (iota((rows, WIDTH), 0) & 3) < new_ref[...]
    attention = jnp.where(used, weighted / total, 0.0).astype(BF16)
    terms = jnp.dot(attention, w_ref[...], preferred_element_type=F32).astype(BF16)
    for s in range(w_ref.shape[1] // WIDTH):
        out_ref[s * rows : (s + 1) * rows] = terms[:, s * WIDTH : (s + 1) * WIDTH]


def local(
    tokens,
    norm_gain,
    w_qkv,
    w_out,
    root_kv,
    branch_kv,
    leaf_kv,
    branch,
    node_owner,
    branch_len,
    leaf_len,
    new_count,
):
    rows = tokens.shape[0]
    nodes = node_owner.shape[0]
    tensor = w_out.shape[1] // WIDTH
    column = lax.axis_size("z")
    plane = nodes // column

    def call(kernel, name, out_shape, specs, outs, scratch=(), **extra):
        return pl.pallas_call(
            kernel,
            out_shape=out_shape,
            in_specs=specs,
            out_specs=outs,
            scratch_shapes=scratch,
            compiler_params=PARAMS,
            name=name,
            **extra,
        )

    def after(first, value):
        return lax.optimization_barrier((first, value))[1]

    def swap(value, axis, distance):
        size = lax.axis_size(axis)
        return lax.ppermute(value, axis, [(i, i ^ distance) for i in range(size)])

    gain = norm_gain[None]
    weights = w_qkv.transpose(1, 0, 2)
    me = lax.axis_index("z").reshape(1)
    q, sent = call(
        front_kernel,
        "front",
        [sds(rows, BF16), sds(column * PACK, BF16)],
        [HB] * 5,
        [VM] * 2,
        [
            pltpu.SMEM((rows // DRAFTS,), jnp.int32),
            pltpu.SMEM((nodes,), jnp.int32),
            pltpu.VMEM(tokens.shape, BF16),
            pltpu.VMEM(gain.shape, F32),
            pltpu.VMEM(weights.shape[1:], BF16),
            pltpu.SMEM((nodes,), jnp.int32),
            pltpu.SemaphoreType.DMA((5,)),
        ],
    )(*[pltpu.with_memory_space_constraint(a, pltpu.HBM) for a in (branch[:, 0], node_owner, tokens, gain, weights)])
    got = lax.all_to_all(sent, "z", 0, 0, tiled=True)
    root_rows = after(sent, root_kv.reshape(-1, WIDTH))
    pair = jnp.concatenate([root_rows, after(got, swap(root_rows, "x", 1))], axis=0)
    asked = call(
        select_kernel, "select", sds(plane * 64, BF16), [SM, VM], VM
    )(me, got)
    incoming = lax.all_to_all(asked, ("x", "c"), 0, 0, tiled=True)
    far = swap(pair, "x", 2)
    answer = call(
        branch_kernel,
        "branch",
        sds(plane * PACK, BF16),
        [SM] + [VM] * 5,
        HB,
        [pltpu.VMEM((2, plane * PACK // 2, WIDTH), BF16), pltpu.SemaphoreType.DMA((2,))],
        cost_estimate=pl.CostEstimate(flops=5000000000, transcendentals=0, bytes_accessed=0),
    )(
        lax.axis_index(REQ).reshape(1),
        node_owner[None],
        branch_len[None],
        incoming,
        branch_kv[0, :, 0],
        branch_kv[0, :, 1].T,
    )
    back = lax.all_to_all(answer, ("x", "c"), 0, 0, tiled=True)
    quad = jnp.concatenate([pair, after(answer, far)], axis=0)
    near = swap(quad, "c", 1)
    root_mean, root_level = call(
        root_kernel,
        "root",
        [sds(column * 64, F32)] * 2,
        [VM] * 3,
        [VM] * 2,
    )(got, quad, near)
    merged = call(
        merge_kernel,
        "merge",
        sds(column * PACK, BF16),
        [SM] + [VM] * 4,
        VM,
    )(me, got, back, root_mean, root_level)
    parts = lax.all_to_all(merged, "z", 0, 0, tiled=True)
    m_local, t_local, o_local, new_row = call(
        local_kernel,
        "local",
        [sds(rows, F32)] * 3 + [sds(rows, jnp.int32)],
        [SM] * 2 + [VM] * 6,
        [VM] * 4,
    )(
        leaf_len,
        new_count,
        tokens,
        gain,
        weights,
        after(merged, q),
        leaf_kv[:, :, 0].reshape(-1, WIDTH),
        leaf_kv[:, :, 1].reshape(-1, WIDTH),
    )
    terms = call(
        finish_kernel, "finish", sds(tensor * rows, BF16), [VM] * 6, VM
    )(parts, new_row, m_local, t_local, o_local, w_out)
    shares = lax.all_to_all(terms, "y", 0, 0, tiled=True)
    return jnp.sum(shares.reshape(tensor, rows, WIDTH).astype(F32), axis=0).astype(BF16)


def solution(mesh):
    split = Mesh(mesh.devices.reshape(8, 4, 2, 8), REQ + ("y",))
    placed = (
        P(REQ, None),
        P(),
        P(None, None, "y"),
        P("y", None),
        P(REQ, None, "y"),
        P(REQ, None, None, "y"),
        P(REQ, None, None, "y"),
        P(REQ, None),
        P(),
        P(),
        P(REQ),
        P(REQ),
    )
    return jax.shard_map(
        local, mesh=split, in_specs=placed, out_specs=P(REQ, "y"), check_vma=False
    )
```

```python
import jax
import jax.numpy as jnp
from jax import lax
from jax.experimental import pallas as pl
from jax.experimental.pallas import tpu as pltpu
from jax.sharding import Mesh
from jax.sharding import PartitionSpec as P

HD = 64
WIDTH = 128
DRAFTS = 4
CAPACITY = 2
PACK = 72
NEG = -1e30
F32 = jnp.float32
BF16 = jnp.bfloat16
REQ = ("z", "x", "c")
VM = pl.BlockSpec(memory_space=pltpu.VMEM)
SM = pl.BlockSpec(memory_space=pltpu.SMEM)
HB = pl.BlockSpec(memory_space=pltpu.HBM)
PARAMS = pltpu.CompilerParams(vmem_limit_bytes=48 * 1024 * 1024)


def iota(shape, dim):
    return lax.broadcasted_iota(jnp.int32, shape, dim)


def low_lanes(shape):
    return iota(shape, len(shape) - 1) < HD


def stack_heads(q):
    low = low_lanes(q.shape)
    zero = jnp.zeros_like(q)
    return jnp.concatenate([jnp.where(low, q, zero), jnp.where(low, zero, q)], axis=0)


def merge_heads(x):
    n = x.shape[0] // 2
    return jnp.where(low_lanes((n, WIDTH)), x[:n], x[n:])


def dot_nt(a, b):
    return lax.dot_general(a, b, (((1,), (1,)), ((), ())), preferred_element_type=F32)


def sds(rows, dtype):
    return jax.ShapeDtypeStruct((rows, WIDTH), dtype)


def places_of(branch_s, owner_s, count_s, requests):
    targets = [owner_s[branch_s[r]] for r in range(requests)]
    for r in range(requests):
        count_s[targets[r]] = 0
    places = []
    for r in range(requests):
        earlier = count_s[targets[r]]
        count_s[targets[r]] = earlier + 1
        places.append(targets[r] * CAPACITY + earlier)
    return places


def local_group(q, own_k, own_v, leaf_k, leaf_v, leaf_row, new_row):
    rows = q.shape[0]
    stacked = stack_heads(q)
    leaf_two = jnp.concatenate([leaf_row, leaf_row], axis=0)
    new_two = jnp.concatenate([new_row, new_row], axis=0)
    both = 2 * rows
    span = leaf_k.shape[0]
    score_leaf = dot_nt(stacked, leaf_k)
    score_own = dot_nt(stacked, own_k)
    key = iota((both, span), 1)
    request_of = (iota((both, span), 0) & (rows - 1)) >> 2
    leaf_wide = jnp.concatenate([leaf_two] * (span // WIDTH), axis=1)
    ok_leaf = ((key >> 4) == request_of) & ((key & 15) < leaf_wide)
    key = iota((both, rows), 1)
    query = iota((both, rows), 0) & (rows - 1)
    ok_own = (
        ((key >> 2) == (query >> 2))
        & ((key & 3) <= (query & 3))
        & ((key & 3) < new_two[:, :rows])
    )
    score_leaf = jnp.where(ok_leaf, score_leaf, NEG)
    score_own = jnp.where(ok_own, score_own, NEG)
    peak = jnp.maximum(
        jnp.max(score_leaf, axis=1, keepdims=True), jnp.max(score_own, axis=1, keepdims=True)
    )
    w_leaf = jnp.where(ok_leaf, jnp.exp(score_leaf - peak), 0.0)
    w_own = jnp.where(ok_own, jnp.exp(score_own - peak), 0.0)
    total = jnp.sum(w_leaf, axis=1, keepdims=True) + jnp.sum(w_own, axis=1, keepdims=True)
    weighted = jnp.dot(w_leaf.astype(BF16), leaf_v, preferred_element_type=F32) + jnp.dot(
        w_own.astype(BF16), own_v, preferred_element_type=F32
    )
    return (
        merge_heads(jnp.broadcast_to(peak, (both, WIDTH))),
        merge_heads(jnp.broadcast_to(total, (both, WIDTH))),
        merge_heads(weighted),
    )


def normed_rows(tok_ref, gain_ref):
    x = tok_ref[...].astype(F32)
    scale = lax.rsqrt(jnp.mean(x * x, axis=1, keepdims=True) + 1e-05)
    return (x * scale * gain_ref[...]).astype(BF16)


def front_kernel(
    me_s, branch_hbm, owner_hbm, tok_hbm, gain_hbm, w_hbm, node_hbm, len_hbm,
    q_ref, out_ref, owned_ref,
    branch_s, owner_s, tok_ref, gain_ref, w_ref, node_ref, len_ref, count_s, sem,
):
    rows = tok_ref.shape[0]
    requests = rows // DRAFTS
    pairs = (
        (branch_hbm, branch_s),
        (owner_hbm, owner_s),
        (tok_hbm, tok_ref),
        (gain_hbm, gain_ref),
        (w_hbm.at[0], w_ref),
        (node_hbm, node_ref),
        (len_hbm, len_ref),
    )
    fetches = [pltpu.make_async_copy(a, b, sem.at[n]) for n, (a, b) in enumerate(pairs)]
    for fetch in fetches:
        fetch.start()
    fetches[0].wait()
    fetches[1].wait()
    places = places_of(branch_s, owner_s, count_s, requests)
    lane = iota((8, WIDTH), 1) >> 2
    slots = jnp.zeros((8, WIDTH), jnp.int32)
    for r in range(requests):
        slots = jnp.where(lane == r, places[r], slots)
    fetches[2].wait()
    fetches[3].wait()
    normed = normed_rows(tok_ref, gain_ref)
    fetches[5].wait()
    fetches[6].wait()
    length = jnp.where(node_ref[...] == me_s[0], len_ref[...], 0)
    owned_ref[...] = jnp.broadcast_to(jnp.sum(length, axis=1, keepdims=True), owned_ref.shape)
    fetches[4].wait()
    q = jnp.dot(normed, w_ref[...], preferred_element_type=F32).astype(BF16)
    q = q * jnp.asarray(HD**-0.5, BF16)
    q_ref[...] = q
    block = jnp.concatenate([q.astype(F32), slots.astype(F32)], axis=0)
    out_ref[...] = jnp.concatenate([block] * (out_ref.shape[0] // PACK), axis=0).astype(BF16)


def routes(got, me):
    found = []
    for s in range(got.shape[0]):
        place = jnp.broadcast_to(got[s, 64:72][:1, :64], (64, 64)).astype(jnp.int32)
        at = ((place >> 1) & 7) * 8 + (place & 1) * DRAFTS + (iota((64, 64), 1) & 3)
        here = ((place >> 4) == me) & (iota((64, 64), 0) == at)
        found.append(jnp.where(here, 1.0, 0.0))
    return found


def select_kernel(me_s, got_ref, out_ref):
    planes = out_ref.shape[0] // 64
    got = got_ref[...].astype(F32).reshape(-1, PACK, WIDTH)
    chosen = [
        jnp.dot(
            route.astype(BF16), got[s, :64].astype(BF16), preferred_element_type=F32
        ).reshape(planes, 8, WIDTH)
        for s, route in enumerate(routes(got, me_s[0]))
    ]
    out_ref[...] = jnp.concatenate(chosen, axis=1).reshape(-1, WIDTH).astype(BF16)


def attend(blocks, keys, values_t, valid):
    count = blocks[0].shape[0]
    first = iota((WIDTH, count), 0) < HD
    scores = [dot_nt(keys, stack_heads(q)) for q in blocks]
    if valid is not None:
        scores = [jnp.where(valid, score, NEG) for score in scores]
    peaks = [jnp.max(score, axis=0, keepdims=True) for score in scores]
    weights, totals = [], []
    for score, peak in zip(scores, peaks):
        weight = jnp.exp(score - peak)
        totals.append(jnp.sum(weight, axis=0, keepdims=True))
        weights.append(weight.astype(BF16))
    for weight, peak, total in zip(weights, peaks, totals):
        mean = jnp.dot(values_t, weight, preferred_element_type=F32) / total
        mean = jnp.where(first, mean[:, :count], mean[:, count:]).T
        yield mean, peak + jnp.log(total)


def three_terms(level, term):
    one = level.astype(BF16).astype(F32)
    two = (level - one).astype(BF16).astype(F32)
    three = level - one - two
    return jnp.where(term == 0, one, jnp.where(term == 1, two, jnp.where(term == 2, three, 0.0)))


def own_lanes(shape):
    return (iota(shape, 1) >> 4) == (iota(shape, 0) & 7)


def level_sum(second):
    row, column = iota((WIDTH, WIDTH), 0), iota((WIDTH, WIDTH), 1)
    head = ((row >> 3) & 1) == (column >> 6)
    term = (row & 7) == 3 if second else (row & 7) < 3
    return jnp.where(head & term, 1.0, 0.0).astype(BF16)


def branch_kernel(len_ref, q_ref, k_ref, vt_ref, out_hbm, out_ref, sem):
    span = k_ref.shape[0]
    block = 256
    size = block // 64 * PACK
    valid = iota((span, 2 * block), 0) < len_ref[:1, :1]
    to = iota((size, 2 * block), 0)
    frm = iota((size, 2 * block), 1)
    query = frm & (block - 1)
    goal = (query >> 6) * PACK + jnp.where(frm < block, query & 63, 64 + ((query >> 3) & 7))
    spread = jnp.where(to == goal, 1.0, 0.0).astype(BF16)
    repeat = jnp.where((iota((16, WIDTH), 1) & 15) == iota((16, WIDTH), 0), 1.0, 0.0).astype(BF16)
    mine = own_lanes((block, WIDTH))
    term = iota((8, 2 * block), 0)
    blocks = [q_ref[b * block : (b + 1) * block] for b in range(q_ref.shape[0] // block)]
    sends = []
    for b, (mean, level) in enumerate(attend(blocks, k_ref[...], vt_ref[...], valid)):
        terms = jnp.where(term == 3, 1.0, three_terms(level, term))
        terms = jnp.concatenate([terms[:, :block], terms[:, block:]], axis=0).astype(BF16)
        levels = lax.dot_general(
            terms, repeat, (((0,), (0,)), ((), ())), preferred_element_type=F32
        )
        levels = jnp.where(mine, levels, 0.0)
        packed = jnp.dot(
            spread, jnp.concatenate([mean, levels], axis=0).astype(BF16), preferred_element_type=F32
        )
        out_ref[b] = packed.astype(BF16)
        sends.append(
            pltpu.make_async_copy(out_ref.at[b], out_hbm.at[pl.ds(b * size, size)], sem.at[b])
        )
        sends[b].start()
    for send in sends:
        send.wait()


def root_kernel(got_ref, rows_ref, more_ref, mean_ref, level_ref):
    sort = (iota((128, 128), 0) & 63) * 2 + (iota((128, 128), 0) >> 6) == iota((128, 128), 1)
    sort = jnp.where(sort, 1.0, 0.0).astype(BF16)
    wide = jnp.concatenate(
        [ref[s : s + 128] for ref in (rows_ref, more_ref) for s in range(0, ref.shape[0], 128)],
        axis=1,
    )
    kinds = jnp.dot(sort, wide, preferred_element_type=F32)
    keys, values = (
        jnp.concatenate(
            [kinds[r : r + 64, s : s + WIDTH] for s in range(0, wide.shape[1], WIDTH)], axis=0
        )
        for r in (0, 64)
    )
    got = got_ref[...].astype(F32).reshape(-1, PACK, WIDTH)
    block = 256
    q = got[:, :64].reshape(-1, WIDTH).astype(BF16)
    blocks = [q[s : s + block] for s in range(0, q.shape[0], block)]
    first = iota((WIDTH, block), 0) < HD
    found = attend(blocks, keys.astype(BF16), values.T.astype(BF16), None)
    for b, (mean, level) in enumerate(found):
        mean_ref[b * block : (b + 1) * block] = mean
        level_ref[b * block : (b + 1) * block] = jnp.where(
            first, level[:, :block], level[:, block:]
        ).T


def merge_kernel(me_s, got_ref, back_ref, mean_ref, level_ref, out_ref):
    got = got_ref[...].astype(F32).reshape(-1, PACK, WIDTH)
    back = back_ref[...].astype(F32).reshape(-1, PACK, WIDTH)
    planes = back.shape[0]
    mine = own_lanes((64, WIDTH))
    picked = []
    for s, route in enumerate(routes(got, me_s[0])):
        part = back[:, s * 8 : s * 8 + 8].reshape(64, WIDTH)
        shared = jnp.broadcast_to(back[:, 64 + s : 65 + s], (planes, 8, WIDTH)).reshape(64, WIDTH)
        both = jnp.concatenate([part, jnp.where(mine, shared, 0.0)], axis=1).astype(BF16)
        picked.append(jnp.dot(route.T.astype(BF16), both, preferred_element_type=F32))
    picked = jnp.concatenate(picked, axis=0)
    part = picked[:, :WIDTH]
    sums = jnp.dot(
        picked[:, WIDTH:].astype(BF16),
        jnp.concatenate([level_sum(False), level_sum(True)], axis=1),
        preferred_element_type=F32,
    )
    level = jnp.where(sums[:, WIDTH:] > 0.5, sums[:, :WIDTH], NEG)
    high = jnp.maximum(level, level_ref[...])
    scale_root = jnp.exp(level_ref[...] - high)
    scale_branch = jnp.exp(level - high)
    total = scale_root + scale_branch
    mean = (mean_ref[...] * scale_root + part * scale_branch) / total
    level = high + jnp.log(total)
    lane = iota(level.shape, 1)
    level = jnp.where(((lane >> 3) & 1) == 0, level[:, :1], level[:, HD : HD + 1])
    levels = jnp.where(own_lanes(level.shape), three_terms(level, lane & 7), 0.0)
    levels = jnp.sum(levels.reshape(-1, 8, WIDTH), axis=1).reshape(-1, 8, WIDTH)
    packed = jnp.concatenate([mean.reshape(-1, 64, WIDTH), levels], axis=1)
    out_ref[...] = packed.reshape(-1, WIDTH).astype(BF16)


def local_kernel(
    leaf_len_s, new_s, tok_ref, gain_ref, w_ref, q_ref, leaf_k_ref, leaf_v_ref, m_ref, t_ref, o_ref, new_ref
):
    rows = tok_ref.shape[0]
    row = iota((rows, WIDTH), 0)
    leaf_row = jnp.zeros((rows, WIDTH), jnp.int32)
    new_row = jnp.zeros((rows, WIDTH), jnp.int32)
    for r in range(rows // DRAFTS):
        mine = (row >> 2) == r
        leaf_row = jnp.where(mine, leaf_len_s[r], leaf_row)
        new_row = jnp.where(mine, new_s[r], new_row)
    new_ref[...] = new_row
    normed = normed_rows(tok_ref, gain_ref)

    def project(n):
        return jnp.dot(normed, w_ref[n], preferred_element_type=F32).astype(BF16)

    m_ref[...], t_ref[...], o_ref[...] = local_group(
        q_ref[...], project(1), project(2), leaf_k_ref[...], leaf_v_ref[...], leaf_row, new_row
    )


def finish_kernel(parts_ref, new_ref, m_ref, t_ref, o_ref, w_ref, out_ref):
    rows = new_ref.shape[0]
    parts = parts_ref[...].astype(F32).reshape(-1, PACK, WIDTH)
    count = parts.shape[0]
    shared = jnp.broadcast_to(parts[:, 64:, None], (count, 8, 8, WIDTH)).reshape(-1, WIDTH)
    shared = jnp.where(own_lanes(shared.shape), shared, 0.0).astype(BF16)
    levels = jnp.dot(shared, level_sum(False), preferred_element_type=F32).reshape(count, rows, WIDTH)
    high = jnp.maximum(jnp.max(levels, axis=0), m_ref[...])
    scale = jnp.exp(m_ref[...] - high)
    total = t_ref[...] * scale
    weighted = o_ref[...] * scale
    for s in range(count):
        scale = jnp.exp(levels[s] - high)
        total = total + scale
        weighted = weighted + parts[s, :64] * scale
    used = (iota((rows, WIDTH), 0) & 3) < new_ref[...]
    attention = jnp.where(used, weighted / total, 0.0).astype(BF16)
    terms = jnp.dot(attention, w_ref[...], preferred_element_type=F32).astype(BF16)
    for s in range(w_ref.shape[1] // WIDTH):
        out_ref[s * rows : (s + 1) * rows] = terms[:, s * WIDTH : (s + 1) * WIDTH]


def local(
    tokens,
    norm_gain,
    w_qkv,
    w_out,
    root_kv,
    branch_kv,
    leaf_kv,
    branch,
    node_owner,
    branch_len,
    leaf_len,
    new_count,
):
    rows = tokens.shape[0]
    nodes = node_owner.shape[0]
    tensor = w_out.shape[1] // WIDTH
    column = lax.axis_size("z")
    plane = nodes // column

    def call(kernel, name, out_shape, specs, outs, scratch=(), **extra):
        return pl.pallas_call(
            kernel,
            out_shape=out_shape,
            in_specs=specs,
            out_specs=outs,
            scratch_shapes=scratch,
            compiler_params=PARAMS,
            name=name,
            **extra,
        )

    def after(first, value):
        return lax.optimization_barrier((first, value))[1]

    def swap(value, axis, distance):
        size = lax.axis_size(axis)
        return lax.ppermute(value, axis, [(i, i ^ distance) for i in range(size)])

    gain = norm_gain[None]
    weights = w_qkv.transpose(1, 0, 2)
    me = lax.axis_index("z").reshape(1)
    q, sent, owned = call(
        front_kernel,
        "front",
        [sds(rows, BF16), sds(column * PACK, BF16), sds(8, jnp.int32)],
        [SM] + [HB] * 7,
        [VM] * 3,
        [
            pltpu.SMEM((rows // DRAFTS,), jnp.int32),
            pltpu.SMEM((nodes,), jnp.int32),
            pltpu.VMEM(tokens.shape, BF16),
            pltpu.VMEM(gain.shape, F32),
            pltpu.VMEM(weights.shape[1:], BF16),
            pltpu.VMEM((1, nodes), jnp.int32),
            pltpu.VMEM((1, nodes), jnp.int32),
            pltpu.SMEM((nodes,), jnp.int32),
            pltpu.SemaphoreType.DMA((7,)),
        ],
    )(
        lax.axis_index(REQ).reshape(1),
        *[
            pltpu.with_memory_space_constraint(a, pltpu.HBM)
            for a in (
                branch[:, 0], node_owner, tokens, gain, weights, node_owner[None], branch_len[None]
            )
        ],
    )
    got = lax.all_to_all(sent, "z", 0, 0, tiled=True)
    root_rows = after(sent, root_kv.reshape(-1, WIDTH))
    pair = jnp.concatenate([root_rows, after(got, swap(root_rows, "x", 1))], axis=0)
    asked = call(
        select_kernel, "select", sds(plane * 64, BF16), [SM, VM], VM
    )(me, got)
    incoming = lax.all_to_all(asked, ("x", "c"), 0, 0, tiled=True)
    far = swap(pair, "x", 2)
    answer = call(
        branch_kernel,
        "branch",
        sds(plane * PACK, BF16),
        [VM] * 4,
        HB,
        [pltpu.VMEM((2, plane * PACK // 2, WIDTH), BF16), pltpu.SemaphoreType.DMA((2,))],
        cost_estimate=pl.CostEstimate(flops=5000000000, transcendentals=0, bytes_accessed=0),
    )(
        owned,
        incoming,
        branch_kv[0, :, 0],
        branch_kv[0, :, 1].T,
    )
    back = lax.all_to_all(answer, ("x", "c"), 0, 0, tiled=True)
    quad = jnp.concatenate([pair, after(answer, far)], axis=0)
    near = swap(quad, "c", 1)
    root_mean, root_level = call(
        root_kernel,
        "root",
        [sds(column * 64, F32)] * 2,
        [VM] * 3,
        [VM] * 2,
    )(got, quad, near)
    merged = call(
        merge_kernel,
        "merge",
        sds(column * PACK, BF16),
        [SM] + [VM] * 4,
        VM,
    )(me, got, back, root_mean, root_level)
    parts = lax.all_to_all(merged, "z", 0, 0, tiled=True)
    m_local, t_local, o_local, new_row = call(
        local_kernel,
        "local",
        [sds(rows, F32)] * 3 + [sds(rows, jnp.int32)],
        [SM] * 2 + [VM] * 6,
        [VM] * 4,
    )(
        leaf_len,
        new_count,
        tokens,
        gain,
        weights,
        after(merged, q),
        leaf_kv[:, :, 0].reshape(-1, WIDTH),
        leaf_kv[:, :, 1].reshape(-1, WIDTH),
    )
    terms = call(
        finish_kernel, "finish", sds(tensor * rows, BF16), [VM] * 6, VM
    )(parts, new_row, m_local, t_local, o_local, w_out)
    shares = lax.all_to_all(terms, "y", 0, 0, tiled=True)
    return jnp.sum(shares.reshape(tensor, rows, WIDTH).astype(F32), axis=0).astype(BF16)


def solution(mesh):
    split = Mesh(mesh.devices.reshape(8, 4, 2, 8), REQ + ("y",))
    placed = (
        P(REQ, None),
        P(),
        P(None, None, "y"),
        P("y", None),
        P(REQ, None, "y"),
        P(REQ, None, None, "y"),
        P(REQ, None, None, "y"),
        P(REQ, None),
        P(),
        P(),
        P(REQ),
        P(REQ),
    )
    return jax.shard_map(
        local, mesh=split, in_specs=placed, out_specs=P(REQ, "y"), check_vma=False
    )
```
